256 devices in a mesh: pair: 32 (over z, y), red: 8 (over x, core).
Axes of the slice: x: 4, y: 4, z: 8, core: 2. Of those that a mesh axis runs over, the one named last changes fastest.
Arguments:
- amplitudes: bfloat16 [2048, 512, 640], P('pair', 'red'), may hold values from -6 to 6
- cycle_integrals: bfloat16 [640, 640], P('pair'), may hold values from -0.5 to 0.5
- ladder_integrals: bfloat16 [32, 8, 1280, 512], P('pair', 'red'), may hold values from -0.125 to 0.125
- orbital_irrep: int32 [640], replicated, may hold values from 0 to 7, as said below
- pair_irrep: int32 [2048], P('pair'), may hold values from 0 to 7, as said below
- tile_owners: int32 [8, 320], replicated, may hold values from 0 to 319, each once within a row
- ladder_tiles: int32 [32, 4], replicated, may hold values from 0 to 2559
Outputs:
- ladder_block: bfloat16 [32, 2048, 512], P('pair', 'red')
The draws below stay inside these ranges and needn't reach their ends.
Inputs may be any that keep to these rules, and one draw needn't show every extreme that they name: Each row of tile_owners is a permutation of 0 .. 319. `orbital_irrep`: nondecreasing along the virtual orbitals; the first is 0 and the last 7. A program must be right for any labels meeting these rules, including one irrep holding nearly all orbitals. `pair_irrep`: A program must be right for any labels in the range, in any mixture.
All inputs are finite; a program needn't handle non-finite values.
Results may differ from the reference program's by a relative error of at most 0.019.
Values may be sent and summed in bfloat16 or wider, within the bound.
A program may use at most 128 MiB of HBM per device.

```python
import jax
import jax.numpy as jnp
from jax import lax

NV = 640
NA = 512
NIRREP = 8
LAB = 512
NOP = 2048
TPR = 320
TPO = 10
LT = 4
N_PAIR = 32
N_RED = 8


def draw_orbital_irrep(key, part):
    first_key, second_key = jax.random.split(jax.random.fold_in(key, 17))
    common = jax.random.randint(first_key, (NV,), 0, 10)
    others = jax.random.randint(second_key, (NV,), 1, NIRREP)
    labels = jnp.where(common < 7, 0, others).astype(jnp.int32)
    labels = jnp.sort(labels).astype(jnp.int32)
    labels = labels.at[0].set(0).at[NV - 1].set(NIRREP - 1)
    return labels.astype(jnp.int32)


def draw_pair_irrep(key, part):
    first_key, second_key = jax.random.split(jax.random.fold_in(key, 29))
    common = jax.random.randint(first_key, (NOP,), 0, 4)
    others = jax.random.randint(second_key, (NOP,), 1, NIRREP)
    return jnp.where(common < 3, 0, others).astype(jnp.int32)


def set_ends(result, rng, smallest, largest):
    dims = result.shape
    spot = [jax.random.randint(jax.random.fold_in(rng, axis), (), 0, dims[axis]) for axis in range(len(dims))]
    result = result.at[tuple(spot)].set(smallest)
    longest = dims.index(max(dims))
    spot[longest] = (spot[longest] + 1) % dims[longest]
    return result.at[tuple(spot)].set(largest)


def block_levels(key, extent, pieces, smallest, largest):
    level = 1.0
    for axis_at, parts in pieces:
        heights = jax.random.uniform(jax.random.fold_in(jax.random.fold_in(key, 6), axis_at), (parts,), jnp.float32, smallest / len(pieces), largest / len(pieces))
        level = level * jnp.repeat(jnp.exp(heights), extent[axis_at] // parts).reshape((-1,) + (1,) * (len(extent) - 1 - axis_at))
    return level


def noise(own_key, shape, spread, most, cuts=(), kind=jnp.bfloat16):
    values = jax.random.normal(own_key, shape, jnp.float32) * spread
    if len(cuts) > 0:
        values = block_levels(own_key, shape, cuts, -0.22, 0.18) * values
    return jnp.clip(values, min=-most, max=most).astype(kind)


def setup_inputs(seed: int = 0) -> dict:
    arg_keys = jax.random.split(jax.random.key(seed), 8)
    amplitudes = noise(arg_keys[0], (NOP, NA, NV), 1.0, 6.0, ((0, 32), (1, 8)))
    cycle_integrals = noise(arg_keys[1], (NV, NV), (NV // 4) ** -0.5, 0.5, ((0, 32),))
    ladder_integrals = noise(arg_keys[2], (N_PAIR, N_RED, TPO * 128, LAB), (N_RED * TPO * 32) ** -0.5, 0.125, ((0, 32), (1, 8)))
    orbital_irrep = draw_orbital_irrep(jax.random.fold_in(arg_keys[7], 71), 0)
    pair_irrep = draw_pair_irrep(jax.random.fold_in(arg_keys[7], 71), 0)
    tile_owners = jax.vmap(lambda own: jax.random.permutation(own, TPR))(jax.random.split(arg_keys[5], N_RED)).reshape((N_RED, TPR)).astype(jnp.int32)
    ladder_tiles = set_ends(jax.random.randint(arg_keys[6], (N_PAIR, LT), 0, NA * (NV // 128)), jax.random.fold_in(arg_keys[6], 1), 0, (NA * (NV // 128)) - 1).astype(jnp.int32)
    return dict(amplitudes=amplitudes, cycle_integrals=cycle_integrals, ladder_integrals=ladder_integrals, orbital_irrep=orbital_irrep, pair_irrep=pair_irrep, tile_owners=tile_owners, ladder_tiles=ladder_tiles)


def reference(amplitudes, cycle_integrals, ladder_integrals, orbital_irrep, pair_irrep, tile_owners, ladder_tiles):
    block_count = NV // 128
    slab_rows = NA // N_RED
    irrep_a = orbital_irrep[:NA]
    allowed = jnp.bitwise_xor(irrep_a[:, None], orbital_irrep[None, :])[None] == pair_irrep[:, None, None]
    symmetric = jnp.where(allowed, amplitudes, jnp.zeros_like(amplitudes))
    cycle_keep = orbital_irrep[:, None] == orbital_irrep[None, :]
    blocked = jnp.where(cycle_keep, cycle_integrals, jnp.zeros_like(cycle_integrals))
    flattened = symmetric.reshape(-1, NV)
    cycle = jnp.dot(flattened, blocked, preferred_element_type=jnp.float32)
    dressed = (flattened.astype(jnp.float32) + cycle).astype(jnp.bfloat16)
    tiles_all = dressed.reshape(NOP, N_RED, TPR, 128)
    lane_ids = jnp.arange(128, dtype=jnp.int32)
    red_ids = jnp.arange(N_RED, dtype=jnp.int32)

    def owner_block(pair_index):
        mine_tiles = lax.dynamic_slice_in_dim(tile_owners, pair_index * TPO, TPO, 1)
        picked = tiles_all[:, red_ids[:, None], mine_tiles]
        owned = picked.reshape(NOP, N_RED * TPO * 128)
        a_rows = red_ids[:, None] * slab_rows + mine_tiles // block_count
        b_cols = (mine_tiles % block_count)[:, :, None] * 128 + lane_ids
        irrep_cd = jnp.bitwise_xor(orbital_irrep[a_rows][:, :, None], orbital_irrep[b_cols]).reshape(-1)
        batch_ids = ladder_tiles[pair_index]
        a_out = batch_ids // block_count
        b_out = (batch_ids % block_count)[:, None] * 128 + lane_ids
        irrep_ab = jnp.bitwise_xor(orbital_irrep[a_out][:, None], orbital_irrep[b_out]).reshape(-1)
        weights = ladder_integrals[pair_index].reshape(N_RED * TPO * 128, LAB)
        masked = jnp.where(irrep_cd[:, None] == irrep_ab[None, :], weights, jnp.zeros_like(weights))
        return jnp.dot(owned, masked, preferred_element_type=jnp.float32).astype(jnp.bfloat16)

    return lax.map(owner_block, jnp.arange(N_PAIR, dtype=jnp.int32))
```

```python
import jax
import jax.numpy as jnp
from jax import lax
from jax.experimental import pallas as pl
from jax.experimental.pallas import tpu as pltpu
from jax.sharding import PartitionSpec as P

NZ, NY, NR = 8, 4, 8
F32, BF16, I32 = jnp.float32, jnp.bfloat16, jnp.int32
FULL = ((0, 0), (1, 0), (-1, 0), (2, -1), (-2, 1), (2, 0), (-2, 0))
HALF = ((2, -2), (-2, 2))


def wrap(v, n):
    return lax.rem(v + n, n)


def kernel(
    amp_hbm, cyc_ref, lad_hbm, irow_ref, towners, ltiles, oirr, pirr,
    out_ref,
    amp_v, cyc_g, w_stage, w_b, irr_x, irr_c, y_stage, dressed, d_send,
    recv_f, recv_h, wbuf, ob_f, ob_h, rr_f, rr_h, fb_f, fb_h, outb,
    amp_sem, own_sem, c_send, c_recv, w_send, w_recv, a_send, a_recv,
    r_send, r_recv, f_send, f_recv,
):
    pair = lax.axis_index("pair")
    r = lax.axis_index("red")
    z, y = lax.div(pair, NY), lax.rem(pair, NY)

    def dev(zz, yy, rr):
        return (wrap(zz, NZ) * NY + wrap(yy, NY), wrap(rr, NR))

    def remote(src, dst, ssem, rsem, where):
        pltpu.make_async_remote_copy(
            src_ref=src, dst_ref=dst, send_sem=ssem, recv_sem=rsem,
            device_id=where, device_id_type=pl.DeviceIdType.MESH,
        ).start()

    def local(src, dst, sem):
        pltpu.make_async_copy(src, dst, sem).start()

    def await_bytes(ref, sem):
        pltpu.make_async_copy(ref, ref, sem).wait()

    for b in range(4):
        rows = pl.ds(b * 16, 16)
        local(amp_hbm.at[rows], amp_v.at[rows], amp_sem.at[b])
    local(lad_hbm, wbuf.at[2], own_sem)

    bar = pltpu.get_barrier_semaphore()
    me = z * NR + r

    def greet(k, _):
        i = lax.rem(me + k, NZ * NR)
        pl.semaphore_signal(
            bar, inc=1, device_id=dev(lax.div(i, NR), y, lax.rem(i, NR)),
            device_id_type=pl.DeviceIdType.MESH,
        )
        return 0

    lax.fori_loop(1, NZ * NR, greet, 0)
    for dz in range(-2, 3):
        for k in range(1, NY):
            pl.semaphore_signal(
                bar, inc=1, device_id=dev(z + dz, y + k, r),
                device_id_type=pl.DeviceIdType.MESH,
            )
    pl.semaphore_wait(bar, NZ * NR - 1 + 5 * (NY - 1))

    local(cyc_ref, cyc_g.at[y, z], c_recv.at[0])
    for k in (4, 3, 5, 2, 6, 1, 7):
        remote(cyc_ref, cyc_g.at[y, z], c_send.at[0], c_recv.at[0], dev(z + k, y, r))

    for h in range(2):
        rows = pl.ds(h * 640, 640)
        remote(lad_hbm.at[rows], wbuf.at[1, rows], w_send, w_recv.at[1, h], dev(z + 1, y, r))
        remote(lad_hbm.at[rows], wbuf.at[3, rows], w_send, w_recv.at[3, h], dev(z - 1, y, r))

    diag = lax.broadcasted_iota(I32, (128, 128), 0) == lax.broadcasted_iota(I32, (128, 128), 1)
    for k in range(5):
        lab = jnp.broadcast_to(irow_ref[:, k * 128 : (k + 1) * 128], (128, 128))
        col = jnp.sum(jnp.where(diag, lab, 0), axis=1, keepdims=True)
        irr_c[k * 128 : (k + 1) * 128, :] = jnp.broadcast_to(col, (128, 128))
    slab = irr_c[pl.ds(pl.multiple_of(r * 64, 64), 64), :]
    for k in range(5):
        irr_x[:, k * 128 : (k + 1) * 128] = jnp.bitwise_xor(slab, irow_ref[:, k * 128 : (k + 1) * 128])

    await_bytes(cyc_g.at[y], c_recv.at[0])
    for k in (2, 1, 3):
        remote(cyc_g.at[y], cyc_g.at[y], c_send.at[1], c_recv.at[1], dev(z, y + k, r))
    await_bytes(cyc_g.at[pl.ds(0, NY - 1)], c_recv.at[1])

    def forward(h):
        rows = pl.ds(h * 640, 640)
        for a, b, dz in ((1, 0, 1), (3, 4, -1)):
            await_bytes(wbuf.at[a, rows], w_recv.at[a, h])
            remote(wbuf.at[a, rows], wbuf.at[b, rows], w_send, w_recv.at[b, h], dev(z + dz, y, r))

    for p in range(NZ * NY):
        w_stage[p * 20 : p * 20 + 20, :] = cyc_g[p % NY, p // NY][:20, :].astype(F32)

    def mask_w(c, _):
        rows = pl.ds(pl.multiple_of(c * 128, 128), 128)
        for k in range(5):
            cols = slice(k * 128, (k + 1) * 128)
            keep = irr_c[rows, :] == irow_ref[:, cols]
            w_b[rows, cols] = jnp.where(keep, w_stage[rows, cols], 0.0).astype(BF16)
        return 0

    lax.fori_loop(0, 5, mask_w, 0)

    def dress(b, _):
        await_bytes(amp_v.at[pl.ds(0, 16)], amp_sem.at[b])

        def quad(q, _):
            ij = b * 16 + q * 4
            x = amp_v[pl.ds(ij, 4)].reshape(256, 640)
            v = jnp.dot(x, w_b[...], preferred_element_type=F32) + x.astype(F32)
            for e in range(4):
                label = pirr[ij + e]
                at = pl.ds(pl.multiple_of((q * 4 + e) * 64, 64), 64)
                for k in range(5):
                    cols = slice(k * 128, (k + 1) * 128)
                    y_stage[k, at, :] = jnp.where(irr_x[:, cols] == label, v[e * 64 : (e + 1) * 64, cols], 0.0)
            return 0

        lax.fori_loop(0, 4, quad, 0)

        def turn(a, _):
            for k in range(5):
                v = y_stage[k, pl.ds(a, 16, stride=64), :]
                dressed[a * 5 + k, pl.ds(pl.multiple_of(b * 16, 16), 16), :] = v.astype(BF16)
            return 0

        lax.fori_loop(0, 64, turn, 0)
        return 0

    lax.fori_loop(0, 4, dress, 0)
    forward(0)

    def order(delta):
        def one(yy, _):
            first = (wrap(z + delta, NZ) * NY + yy) * 10
            for s in range(10):
                d_send[delta % 8, yy, :, s * 128 : (s + 1) * 128] = dressed[towners[r, first + s]]
            return 0

        lax.fori_loop(0, NY, one, 0)

    mine = pl.ds(pl.multiple_of(y * 64, 64), 64)
    mine_h = pl.ds(pl.multiple_of(y * 32, 32), 32)
    for slot, delta, dz in ((0, 0, 0), (1, 1, 0), (2, -1, 0), (3, 3, 1), (4, -3, -1), (None, 4, 2), (5, 2, 0), (6, -2, 0)):
        order(delta)
        buf = d_send.at[delta % 8]
        if slot is None:
            for k in (2, 1, 3, 0):
                yy = wrap(y + k, NY)
                remote(buf.at[yy, pl.ds(0, 32)], recv_h.at[0, mine_h], a_send, a_recv.at[7], dev(z + 2, yy, r))
                remote(buf.at[yy, pl.ds(32, 32)], recv_h.at[1, mine_h], a_send, a_recv.at[8], dev(z - 2, yy, r))
            continue
        for k in (2, 1, 3, 0):
            yy = wrap(y + k, NY)
            if dz == 0 and k == 0:
                local(buf.at[yy], recv_f.at[slot, mine], a_recv.at[slot])
            else:
                remote(buf.at[yy], recv_f.at[slot, mine], a_send, a_recv.at[slot], dev(z + dz, yy, r))
    forward(1)

    def multiply(x, w, o):
        def cols(n, _):
            at = pl.ds(pl.multiple_of(n * 256, 256), 256)
            o[:, at] = jnp.dot(x[...], w[:, at], preferred_element_type=F32).astype(BF16)
            return 0

        lax.fori_loop(0, 2, cols, 0)

    def scatter(o, rr, n, sem):
        def piece(q):
            return o.at[pl.ds(pl.multiple_of(q * n, n), n)]

        for k in (4, 3, 5, 2, 6, 1, 7):
            q = wrap(r + k, NR)
            remote(piece(q), rr.at[r], r_send, sem, dev(z, y, q))
        local(piece(r), rr.at[r], sem)

    def reduce(item):
        if item < 7:
            (o, s), rr, fb, n = FULL[item], rr_f.at[item], fb_f.at[item], 32
            row = r * 32
        else:
            (o, s), rr, fb, n = HALF[item - 7], rr_h.at[item - 7], fb_h.at[item - 7], 16
            row = lax.div(r, 2) * 64 + lax.rem(r, 2) * 16 + (item - 7) * 32
        await_bytes(rr, r_recv.at[item])
        total = rr[0].astype(F32)
        for q in range(1, NR):
            total = total + rr[q].astype(F32)
        fb[...] = total.astype(BF16)
        rows = outb.at[pl.ds(pl.multiple_of(row, 16), n)]
        level = wrap(z + s, NZ)
        if item == 0:

            @pl.when(level == r)
            def _():
                local(fb, rows, f_recv)

            @pl.when(level != r)
            def _():
                remote(fb, rows, f_send.at[0], f_recv, dev(z + o, y, level))
        else:
            remote(fb, rows, f_send.at[1], f_recv, dev(z + o, y, level))

    ready = {2}

    def item_step(item):
        if item < 7:
            o, x, ob, rr, n = FULL[item][0], recv_f.at[item], ob_f.at[item], rr_f.at[item], 32
        else:
            o, x, ob, rr, n = HALF[item - 7][0], recv_h.at[item - 7], ob_h.at[item - 7], rr_h.at[item - 7], 16
        if item == 0:
            await_bytes(wbuf.at[2], own_sem)
        if o in (2, -2) and o + 2 not in ready:
            ready.add(o + 2)
            for h in range(2):
                await_bytes(wbuf.at[o + 2, pl.ds(h * 640, 640)], w_recv.at[o + 2, h])
        await_bytes(x, a_recv.at[item])
        multiply(x, wbuf.at[o + 2], ob)
        scatter(ob, rr, n, r_recv.at[item])

    todo = (0, 1, 2, 3, 4, 7, 8, 5, 6)
    for at, item in enumerate(todo):
        item_step(item)
        if at:
            reduce(todo[at - 1])
    reduce(todo[-1])

    diag64 = lax.broadcasted_iota(I32, (64, 128), 0) == lax.broadcasted_iota(I32, (64, 128), 1)
    await_bytes(outb, f_recv)
    for j in range(4):
        t = ltiles[pair, j]
        la, bb = oirr[lax.div(t, 5)], lax.rem(t, 5)
        lab = jnp.zeros((1, 128), I32)
        for k in range(5):
            lab = lab + jnp.where(bb == k, irow_ref[:, k * 128 : (k + 1) * 128], 0)
        lab = jnp.bitwise_xor(lab, la).astype(F32)
        for yy in range(NY):
            rowl = cyc_g[yy, r][20:21, 0:128].astype(F32)
            col = jnp.sum(jnp.where(diag64, jnp.broadcast_to(rowl, (64, 128)), 0.0), axis=1, keepdims=True)
            keep = jnp.broadcast_to(col, (64, 128)) == lab
            got = outb[yy * 64 : (yy + 1) * 64, j * 128 : (j + 1) * 128].astype(F32)
            out_ref[yy * 64 : (yy + 1) * 64, j * 128 : (j + 1) * 128] = jnp.where(keep, got, 0.0).astype(BF16)

    await_bytes(cyc_g.at[0, pl.ds(0, NZ - 1)], c_send.at[0])
    await_bytes(cyc_g.at[pl.ds(0, NY - 1)], c_send.at[1])
    await_bytes(wbuf.at[pl.ds(0, 4)], w_send)
    await_bytes(d_send.at[pl.ds(0, 6)], a_send)
    await_bytes(d_send.at[0, pl.ds(0, 3)], a_send)
    await_bytes(rr_f.at[:, pl.ds(0, NR - 1)], r_send)
    await_bytes(rr_h.at[:, pl.ds(0, NR - 1)], r_send)

    @pl.when(z != r)
    def _():
        await_bytes(fb_f.at[0], f_send.at[0])

    await_bytes(fb_f.at[pl.ds(0, 6)], f_send.at[1])
    await_bytes(fb_h, f_send.at[1])


def shards(amplitudes, cycle_integrals, ladder_integrals, orbital_irrep, pair_irrep, tile_owners, ladder_tiles):
    cyc = jnp.zeros((24, 640), BF16)
    cyc = cyc.at[:20].set(cycle_integrals).at[20, :64].set(pair_irrep.astype(BF16))
    hbm = pl.BlockSpec(memory_space=pltpu.MemorySpace.HBM)
    vmem = pl.BlockSpec(memory_space=pltpu.MemorySpace.VMEM)
    smem = pl.BlockSpec(memory_space=pltpu.MemorySpace.SMEM)
    dma = pltpu.SemaphoreType.DMA
    out = pl.pallas_call(
        kernel,
        out_shape=jax.ShapeDtypeStruct((256, 512), BF16),
        in_specs=[hbm, vmem, hbm, vmem, smem, smem, smem, smem],
        out_specs=vmem,
        scratch_shapes=[
            pltpu.VMEM((64, 64, 640), BF16),
            pltpu.VMEM((4, 8, 24, 640), BF16),
            pltpu.VMEM((640, 640), F32),
            pltpu.VMEM((640, 640), BF16),
            pltpu.VMEM((64, 640), I32),
            pltpu.VMEM((640, 128), I32),
            pltpu.VMEM((5, 1024, 128), F32),
            pltpu.VMEM((320, 64, 128), BF16),
            pltpu.VMEM((8, 4, 64, 1280), BF16),
            pltpu.VMEM((7, 256, 1280), BF16),
            pltpu.VMEM((2, 128, 1280), BF16),
            pltpu.VMEM((5, 1280, 512), BF16),
            pltpu.VMEM((7, 256, 512), BF16),
            pltpu.VMEM((2, 128, 512), BF16),
            pltpu.VMEM((7, 8, 32, 512), BF16),
            pltpu.VMEM((2, 8, 16, 512), BF16),
            pltpu.VMEM((7, 32, 512), BF16),
            pltpu.VMEM((2, 16, 512), BF16),
            pltpu.VMEM((256, 512), BF16),
            dma((4,)),
            dma,
            dma((2,)),
            dma((2,)),
            dma,
            dma((5, 2)),
            dma,
            dma((9,)),
            dma,
            dma((9,)),
            dma((2,)),
            dma,
        ],
        compiler_params=pltpu.CompilerParams(
            collective_id=0, has_side_effects=True, vmem_limit_bytes=56 << 20
        ),
        name="ladder",
    )(
        amplitudes,
        cyc,
        ladder_integrals.reshape(1280, 512),
        orbital_irrep.reshape(1, 640),
        tile_owners,
        ladder_tiles,
        orbital_irrep,
        pair_irrep,
    )
    return out[None]


def solution(mesh):
    return jax.shard_map(
        shards,
        mesh=mesh,
        in_specs=(
            P("pair", "red", None),
            P("pair", None),
            P("pair", "red", None, None),
            P(),
            P("pair"),
            P(),
            P(),
        ),
        out_specs=P("pair", "red", None),
        check_vma=False,
    )
```

```python
import jax
import jax.numpy as jnp
from jax import lax
from jax.experimental import pallas as pl
from jax.experimental.pallas import tpu as pltpu
from jax.sharding import PartitionSpec as P

NZ, NY, NR = 8, 4, 8
F32, BF16, I32 = jnp.float32, jnp.bfloat16, jnp.int32
FULL = ((0, 0), (1, 0), (-1, 0), (2, -1), (-2, 1), (2, 0), (-2, 0))
HALF = ((2, -2), (-2, 2))
WAY = (0, 3, -3, 4, 1, -1, 2, -2)
NEAR = {0: 0, 1: 1, -1: 2, 2: 5, -2: 6}
FAR = {3: 0, -3: 1, 4: 2}
TODO = {0: (0,), 1: (1,), -1: (2,), 2: (3, 4, 5), -2: (6, 7, 8)}
WINDOW = 3


def wrap(v, n):
    return lax.rem(v + n, n)


def kernel(
    amp_hbm, cyc_ref, lad_hbm, towners, ltiles, oirr, pirr,
    out_ref,
    amp_v, cyc_g, w_stage, w_b, irow_ref, irr_x, irr_c, y_stage, dressed, d_send,
    recv_f, recv_h, far, wbuf, ob_f, ob_h, rr_f, rr_h, fb_f, fb_h, outb,
    amp_sem, own_sem, c_send, c_recv, w_send, w_recv, a_send, a_recv,
    x_send, x_recv, r_send, r_recv, f_send, f_recv,
):
    pair = lax.axis_index("pair")
    r = lax.axis_index("red")
    z, y = lax.div(pair, NY), lax.rem(pair, NY)

    def dev(zz, yy, rr):
        return (wrap(zz, NZ) * NY + wrap(yy, NY), wrap(rr, NR))

    def remote(src, dst, ssem, rsem, where):
        pltpu.make_async_remote_copy(
            src_ref=src, dst_ref=dst, send_sem=ssem, recv_sem=rsem,
            device_id=where, device_id_type=pl.DeviceIdType.MESH,
        ).start()

    def local(src, dst, sem):
        pltpu.make_async_copy(src, dst, sem).start()

    def await_bytes(ref, sem):
        pltpu.make_async_copy(ref, ref, sem).wait()

    for b in range(4):
        rows = pl.ds(b * 16, 16)
        local(amp_hbm.at[rows], amp_v.at[rows], amp_sem.at[b])
    local(lad_hbm, wbuf.at[2], own_sem)

    bar = pltpu.get_barrier_semaphore()
    me = z * NR + r

    def greet(k, _):
        i = lax.rem(me + k, NZ * NR)
        pl.semaphore_signal(
            bar, inc=1, device_id=dev(lax.div(i, NR), y, lax.rem(i, NR)),
            device_id_type=pl.DeviceIdType.MESH,
        )
        return 0

    lax.fori_loop(1, NZ * NR, greet, 0)
    for k in range(1, NY):
        pl.semaphore_signal(
            bar, inc=1, device_id=dev(z, y + k, r),
            device_id_type=pl.DeviceIdType.MESH,
        )
    irow_ref[...] = cyc_ref[21:22, :].astype(F32).astype(I32)
    diag = lax.broadcasted_iota(I32, (128, 128), 0) == lax.broadcasted_iota(I32, (128, 128), 1)
    for k in range(5):
        lab = jnp.broadcast_to(irow_ref[:, k * 128 : (k + 1) * 128], (128, 128))
        col = jnp.sum(jnp.where(diag, lab, 0), axis=1, keepdims=True)
        irr_c[k * 128 : (k + 1) * 128, :] = jnp.broadcast_to(col, (128, 128))
    slab = irr_c[pl.ds(pl.multiple_of(r * 64, 64), 64), :]
    for k in range(5):
        irr_x[:, k * 128 : (k + 1) * 128] = jnp.bitwise_xor(slab, irow_ref[:, k * 128 : (k + 1) * 128])

    pl.semaphore_wait(bar, NZ * NR - 1 + NY - 1)

    core = lax.rem(r, 2)
    sends = lax.rem(z, 2) == core

    @pl.when(sends)
    def _():
        to = cyc_g.at[y, core, lax.div(z, 2)]
        local(cyc_ref, to, c_recv.at[0])
        for k in (4, 3, 5, 2, 6, 1, 7):
            remote(cyc_ref, to, c_send.at[0], c_recv.at[0], dev(z + k, y, r))

    for h in range(2):
        rows = pl.ds(h * 640, 640)
        remote(lad_hbm.at[rows], wbuf.at[1, rows], w_send, w_recv.at[1, h], dev(z + 1, y, r))
        remote(lad_hbm.at[rows], wbuf.at[3, rows], w_send, w_recv.at[3, h], dev(z - 1, y, r))

    part = cyc_g.at[y, core]
    await_bytes(part, c_recv.at[0])
    for k in (2, 1, 3):
        remote(part, part, c_send.at[1], c_recv.at[1], dev(z, y + k, r))
    await_bytes(cyc_g.at[pl.ds(0, NY - 1), 0], c_recv.at[1])
    part = cyc_g.at[:, core]
    remote(part, part, c_send.at[2], c_recv.at[2], dev(z, y, r + 1 - 2 * core))
    await_bytes(part, c_recv.at[2])

    def forward(h):
        rows = pl.ds(h * 640, 640)
        for a, b, dz in ((1, 0, 1), (3, 4, -1)):
            await_bytes(wbuf.at[a, rows], w_recv.at[a, h])
            remote(wbuf.at[a, rows], wbuf.at[b, rows], w_send, w_recv.at[b, h], dev(z + dz, y, r))

    for p in range(NZ * NY):
        w_stage[p * 20 : p * 20 + 20, :] = cyc_g[p % NY, (p // NY) % 2, p // NY // 2][:20, :].astype(F32)

    def mask_w(c, _):
        rows = pl.ds(pl.multiple_of(c * 128, 128), 128)
        for k in range(5):
            cols = slice(k * 128, (k + 1) * 128)
            keep = irr_c[rows, :] == irow_ref[:, cols]
            w_b[rows, cols] = jnp.where(keep, w_stage[rows, cols], 0.0).astype(BF16)
        return 0

    lax.fori_loop(0, 5, mask_w, 0)

    def dress(b, _):
        await_bytes(amp_v.at[pl.ds(0, 16)], amp_sem.at[b])

        def quad(q, _):
            ij = b * 16 + q * 4
            x = amp_v[pl.ds(ij, 4)].reshape(256, 640)
            v = jnp.dot(x, w_b[...], preferred_element_type=F32) + x.astype(F32)
            for e in range(4):
                label = pirr[ij + e]
                at = pl.ds(pl.multiple_of((q * 4 + e) * 64, 64), 64)
                for k in range(5):
                    cols = slice(k * 128, (k + 1) * 128)
                    y_stage[k, at, :] = jnp.where(irr_x[:, cols] == label, v[e * 64 : (e + 1) * 64, cols], 0.0)
            return 0

        lax.fori_loop(0, 4, quad, 0)

        def turn(c, _):
            at = pl.ds(pl.multiple_of(b * 16, 16), 16)
            got = [y_stage[k, pl.ds(c * 8 + i, 16, stride=64), :].astype(BF16) for i in range(8) for k in range(5)]
            for i in range(40):
                dressed[c * 40 + i, at, :] = got[i]
            return 0

        lax.fori_loop(0, 8, turn, 0)
        return 0

    lax.fori_loop(0, 2, dress, 0)
    forward(0)
    lax.fori_loop(2, 4, dress, 0)

    def order(delta):
        def one(yy, _):
            first = (wrap(z + delta, NZ) * NY + yy) * 10
            for s in range(10):
                d_send[delta % 8, yy, :, s * 128 : (s + 1) * 128] = dressed[towners[r, first + s]]
            return 0

        lax.fori_loop(0, NY, one, 0)

    mine = pl.ds(pl.multiple_of(y * 64, 64), 64)

    def send(delta):
        order(delta)
        buf = d_send.at[delta % 8]
        if delta in FAR:
            to, sem = far.at[FAR[delta], mine], x_recv.at[FAR[delta]]
        else:
            to, sem = recv_f.at[NEAR[delta], mine], a_recv.at[NEAR[delta]]
        local(buf.at[y], to, sem)
        for k in (2, 1, 3):
            yy = wrap(y + k, NY)
            remote(buf.at[yy], to, a_send.at[delta % 8], sem, dev(z, yy, r))

    def sent(delta):
        await_bytes(d_send.at[0, pl.ds(0, NY - 1)], a_send.at[delta % 8])

    def go_on(delta):
        at = FAR[delta]
        await_bytes(far.at[at], x_recv.at[at])
        if delta == 4:
            remote(far.at[at, pl.ds(0, 128)], recv_h.at[0], x_send, a_recv.at[7], dev(z + 2, y, r))
            remote(far.at[at, pl.ds(128, 128)], recv_h.at[1], x_send, a_recv.at[8], dev(z - 2, y, r))
        else:
            remote(far.at[at], recv_f.at[3 + at], x_send, a_recv.at[3 + at], dev(z + 1 - 2 * at, y, r))

    for delta in WAY[:WINDOW]:
        send(delta)
    forward(1)

    def multiply(x, w, o):
        def cols(n, _):
            at = pl.ds(pl.multiple_of(n * 256, 256), 256)
            o[:, at] = jnp.dot(x[...], w[:, at], preferred_element_type=F32).astype(BF16)
            return 0

        lax.fori_loop(0, 2, cols, 0)

    def scatter(o, rr, n, sem):
        def piece(q):
            return o.at[pl.ds(pl.multiple_of(q * n, n), n)]

        for k in (4, 3, 5, 2, 6, 1, 7):
            q = wrap(r + k, NR)
            remote(piece(q), rr.at[r], r_send, sem, dev(z, y, q))
        local(piece(r), rr.at[r], sem)

    def reduce(item):
        if item < 7:
            (o, s), rr, fb, n = FULL[item], rr_f.at[item], fb_f.at[item], 32
            row = r * 32
        else:
            (o, s), rr, fb, n = HALF[item - 7], rr_h.at[item - 7], fb_h.at[item - 7], 16
            row = r * 16 + (item - 7) * 128
        await_bytes(rr, r_recv.at[item])
        total = rr[0].astype(F32)
        for q in range(1, NR):
            total = total + rr[q].astype(F32)
        fb[...] = total.astype(BF16)
        rows = outb.at[pl.ds(pl.multiple_of(row, 16), n)]
        level = wrap(z + s, NZ)
        if item == 0:

            @pl.when(level == r)
            def _():
                local(fb, rows, f_recv)

            @pl.when(level != r)
            def _():
                remote(fb, rows, f_send.at[0], f_recv, dev(z + o, y, level))
        else:
            remote(fb, rows, f_send.at[1], f_recv, dev(z + o, y, level))

    ready = {2}

    def item_step(item):
        if item < 7:
            o, x, ob, rr, n = FULL[item][0], recv_f.at[item], ob_f.at[item], rr_f.at[item], 32
        else:
            o, x, ob, rr, n = HALF[item - 7][0], recv_h.at[item - 7], ob_h.at[item - 7], rr_h.at[item - 7], 16
        if item == 0:
            await_bytes(wbuf.at[2], own_sem)
        if o in (2, -2) and o + 2 not in ready:
            ready.add(o + 2)
            for h in range(2):
                await_bytes(wbuf.at[o + 2, pl.ds(h * 640, 640)], w_recv.at[o + 2, h])
        await_bytes(x, a_recv.at[item])
        multiply(x, wbuf.at[o + 2], ob)
        scatter(ob, rr, n, r_recv.at[item])

    last = None
    for i, delta in enumerate(WAY):
        if i + WINDOW < 8:
            sent(delta)
            send(WAY[i + WINDOW])
        if delta in FAR:
            go_on(delta)
            continue
        for item in TODO[delta]:
            item_step(item)
            if last is not None:
                reduce(last)
            last = item
    reduce(last)

    diag64 = lax.broadcasted_iota(I32, (64, 128), 0) == lax.broadcasted_iota(I32, (64, 128), 1)
    await_bytes(outb, f_recv)
    for j in range(4):
        t = ltiles[j, pair]
        la, bb = oirr[lax.div(t, 5)], lax.rem(t, 5)
        lab = jnp.zeros((1, 128), I32)
        for k in range(5):
            lab = lab + jnp.where(bb == k, irow_ref[:, k * 128 : (k + 1) * 128], 0)
        lab = jnp.bitwise_xor(lab, la).astype(F32)
        for yy in range(NY):
            rowl = cyc_g[yy, core, lax.div(r, 2)][20:21, 0:128].astype(F32)
            col = jnp.sum(jnp.where(diag64, jnp.broadcast_to(rowl, (64, 128)), 0.0), axis=1, keepdims=True)
            keep = jnp.broadcast_to(col, (64, 128)) == lab
            got = outb[yy * 64 : (yy + 1) * 64, j * 128 : (j + 1) * 128].astype(F32)
            out_ref[yy * 64 : (yy + 1) * 64, j * 128 : (j + 1) * 128] = jnp.where(keep, got, 0.0).astype(BF16)

    @pl.when(sends)
    def _():
        await_bytes(cyc_g.at[0, 0], c_send.at[0])
        await_bytes(cyc_g.at[0, 1, pl.ds(0, 3)], c_send.at[0])

    await_bytes(cyc_g.at[pl.ds(0, NY - 1), 0], c_send.at[1])
    await_bytes(cyc_g.at[:, 0], c_send.at[2])
    await_bytes(wbuf.at[pl.ds(0, 4)], w_send)
    for delta in WAY[8 - WINDOW :]:
        sent(delta)
    await_bytes(far, x_send)
    await_bytes(rr_f.at[:, pl.ds(0, NR - 1)], r_send)
    await_bytes(rr_h.at[:, pl.ds(0, NR - 1)], r_send)

    @pl.when(z != r)
    def _():
        await_bytes(fb_f.at[0], f_send.at[0])

    await_bytes(fb_f.at[pl.ds(0, 6)], f_send.at[1])
    await_bytes(fb_h, f_send.at[1])


def shards(amplitudes, cycle_integrals, ladder_integrals, orbital_irrep, pair_irrep, tile_owners, ladder_tiles):
    row = lax.broadcasted_iota(I32, (24, 640), 0)
    cyc = jnp.where(row < 20, jnp.pad(cycle_integrals, ((0, 4), (0, 0))), jnp.zeros((), BF16))
    labels = jnp.pad(pair_irrep, (0, 576))[None, :].astype(BF16)
    cyc = jnp.where(row == 20, labels, cyc)
    cyc = jnp.where(row == 21, orbital_irrep[None, :].astype(BF16), cyc)
    hbm = pl.BlockSpec(memory_space=pltpu.MemorySpace.HBM)
    vmem = pl.BlockSpec(memory_space=pltpu.MemorySpace.VMEM)
    smem = pl.BlockSpec(memory_space=pltpu.MemorySpace.SMEM)
    dma = pltpu.SemaphoreType.DMA
    out = pl.pallas_call(
        kernel,
        out_shape=jax.ShapeDtypeStruct((256, 512), BF16),
        in_specs=[hbm, vmem, hbm, smem, smem, smem, smem],
        out_specs=vmem,
        scratch_shapes=[
            pltpu.VMEM((64, 64, 640), BF16),
            pltpu.VMEM((4, 2, 4, 24, 640), BF16),
            pltpu.VMEM((640, 640), F32),
            pltpu.VMEM((640, 640), BF16),
            pltpu.VMEM((1, 640), I32),
            pltpu.VMEM((64, 640), I32),
            pltpu.VMEM((640, 128), I32),
            pltpu.VMEM((5, 1024, 128), F32),
            pltpu.VMEM((320, 64, 128), BF16),
            pltpu.VMEM((8, 4, 64, 1280), BF16),
            pltpu.VMEM((7, 256, 1280), BF16),
            pltpu.VMEM((2, 128, 1280), BF16),
            pltpu.VMEM((3, 256, 1280), BF16),
            pltpu.VMEM((5, 1280, 512), BF16),
            pltpu.VMEM((7, 256, 512), BF16),
            pltpu.VMEM((2, 128, 512), BF16),
            pltpu.VMEM((7, 8, 32, 512), BF16),
            pltpu.VMEM((2, 8, 16, 512), BF16),
            pltpu.VMEM((7, 32, 512), BF16),
            pltpu.VMEM((2, 16, 512), BF16),
            pltpu.VMEM((256, 512), BF16),
            dma((4,)),
            dma,
            dma((3,)),
            dma((3,)),
            dma,
            dma((5, 2)),
            dma((8,)),
            dma((9,)),
            dma,
            dma((3,)),
            dma,
            dma((9,)),
            dma((2,)),
            dma,
        ],
        compiler_params=pltpu.CompilerParams(
            collective_id=0, has_side_effects=True, vmem_limit_bytes=56 << 20
        ),
        name="ladder",
    )(
        amplitudes,
        cyc,
        ladder_integrals.reshape(1280, 512),
        tile_owners,
        ladder_tiles.T,
        orbital_irrep,
        pair_irrep,
    )
    return out[None]


def solution(mesh):
    return jax.shard_map(
        shards,
        mesh=mesh,
        in_specs=(
            P("pair", "red", None),
            P("pair", None),
            P("pair", "red", None, None),
            P(),
            P("pair"),
            P(),
            P(),
        ),
        out_specs=P("pair", "red", None),
        check_vma=False,
    )
```

```python
import jax
import jax.numpy as jnp
from jax import lax
from jax.experimental import pallas as pl
from jax.experimental.pallas import tpu as pltpu
from jax.sharding import PartitionSpec as P

NZ, NY, NR = 8, 4, 8
F32, BF16, I32 = jnp.float32, jnp.bfloat16, jnp.int32
FULL = ((0, 0), (1, 0), (-1, 0), (2, -1), (-2, 1), (2, 0), (-2, 0))
HALF = ((2, -2), (-2, 2))
WAY = (0, 3, -3, 4, 1, -1, 2, -2)
NEAR = {0: 0, 1: 1, -1: 2, 2: 5, -2: 6}
FAR = {3: 0, -3: 1, 4: 2}
TODO = {0: (0,), 1: (1,), -1: (2,), 2: (3, 4, 5), -2: (6, 7, 8)}
WINDOW = 3


def wrap(v, n):
    return lax.rem(v + n, n)


def kernel(
    amp_hbm, cyc_in, lad_hbm, orow, prow, towners, ltiles, oirr, pirr,
    out_ref,
    amp_v, cyc_ref, cyc_g, w_stage, w_b, irow_ref, irr_x, irr_c, y_stage, dressed, d_send,
    recv_f, recv_h, far, wbuf, ob_f, ob_h, rr_f, rr_h, fb_f, fb_h, outb,
    amp_sem, own_sem, c_send, c_recv, w_send, w_recv, a_send, a_recv,
    x_send, x_recv, r_send, r_recv, f_send, f_recv,
):
    pair = lax.axis_index("pair")
    r = lax.axis_index("red")
    z, y = lax.div(pair, NY), lax.rem(pair, NY)

    def dev(zz, yy, rr):
        return (wrap(zz, NZ) * NY + wrap(yy, NY), wrap(rr, NR))

    def remote(src, dst, ssem, rsem, where):
        pltpu.make_async_remote_copy(
            src_ref=src, dst_ref=dst, send_sem=ssem, recv_sem=rsem,
            device_id=where, device_id_type=pl.DeviceIdType.MESH,
        ).start()

    def local(src, dst, sem):
        pltpu.make_async_copy(src, dst, sem).start()

    def await_bytes(ref, sem):
        pltpu.make_async_copy(ref, ref, sem).wait()

    for b in range(4):
        rows = pl.ds(b * 16, 16)
        local(amp_hbm.at[rows], amp_v.at[rows], amp_sem.at[b])
    local(lad_hbm, wbuf.at[2], own_sem)

    bar = pltpu.get_barrier_semaphore()
    me = z * NR + r

    def greet(k, _):
        i = lax.rem(me + k, NZ * NR)
        pl.semaphore_signal(
            bar, inc=1, device_id=dev(lax.div(i, NR), y, lax.rem(i, NR)),
            device_id_type=pl.DeviceIdType.MESH,
        )
        return 0

    lax.fori_loop(1, NZ * NR, greet, 0)
    for k in range(1, NY):
        pl.semaphore_signal(
            bar, inc=1, device_id=dev(z, y + k, r),
            device_id_type=pl.DeviceIdType.MESH,
        )
    for k in range(5):
        irow_ref[:, k * 128 : (k + 1) * 128] = orow[pl.ds(k * 128, 128)].reshape(1, 128)
    cyc_ref[0:20, :] = cyc_in[...]
    cyc_ref[20:24, :] = jnp.zeros((4, 640), BF16)
    cyc_ref[20:24, 0:64] = jnp.broadcast_to(prow[...].reshape(1, 64), (4, 64)).astype(BF16)
    diag = lax.broadcasted_iota(I32, (128, 128), 0) == lax.broadcasted_iota(I32, (128, 128), 1)
    for k in range(5):
        lab = jnp.broadcast_to(irow_ref[:, k * 128 : (k + 1) * 128], (128, 128))
        col = jnp.sum(jnp.where(diag, lab, 0), axis=1, keepdims=True)
        irr_c[k * 128 : (k + 1) * 128, :] = jnp.broadcast_to(col, (128, 128))
    slab = irr_c[pl.ds(pl.multiple_of(r * 64, 64), 64), :]
    for k in range(5):
        irr_x[:, k * 128 : (k + 1) * 128] = jnp.bitwise_xor(slab, irow_ref[:, k * 128 : (k + 1) * 128])

    pl.semaphore_wait(bar, NZ * NR - 1 + NY - 1)

    side, core = lax.rem(lax.div(r, 2), 2), lax.rem(r, 2)
    sends = lax.rem(z, 4) == lax.rem(r, 4)

    @pl.when(sends)
    def _():
        to = cyc_g.at[side, core, lax.div(z, 4), y]
        local(cyc_ref, to, c_recv.at[0])
        for k in (4, 3, 5, 2, 6, 1, 7):
            remote(cyc_ref, to, c_send.at[0], c_recv.at[0], dev(z + k, y, r))

    for h in range(2):
        rows = pl.ds(h * 640, 640)
        remote(lad_hbm.at[rows], wbuf.at[1, rows], w_send, w_recv.at[1, h], dev(z + 1, y, r))
        remote(lad_hbm.at[rows], wbuf.at[3, rows], w_send, w_recv.at[3, h], dev(z - 1, y, r))

    part = cyc_g.at[side, core, :, y]
    await_bytes(part, c_recv.at[0])
    for k in (2, 1, 3):
        remote(part, part, c_send.at[1], c_recv.at[1], dev(z, y + k, r))
    await_bytes(cyc_g.at[0, 0, :, pl.ds(0, NY - 1)], c_recv.at[1])
    for h, dr in ((0, -2), (1, 2)):
        part = cyc_g.at[side, core, h]
        remote(part, part, c_send.at[2], c_recv.at[2], dev(z, y, r + dr))
    partner = dev(z, y, r + 1 - 2 * core)
    part = cyc_g.at[side, core]
    remote(part, part, c_send.at[3], c_recv.at[3], partner)
    part = cyc_g.at[1 - side, core]
    await_bytes(part, c_recv.at[2])
    remote(part, part, c_send.at[3], c_recv.at[3], partner)
    await_bytes(cyc_g.at[:, 0], c_recv.at[3])

    def forward(h):
        rows = pl.ds(h * 640, 640)
        for a, b, dz in ((1, 0, 1), (3, 4, -1)):
            await_bytes(wbuf.at[a, rows], w_recv.at[a, h])
            remote(wbuf.at[a, rows], wbuf.at[b, rows], w_send, w_recv.at[b, h], dev(z + dz, y, r))

    for p in range(NZ * NY):
        w_stage[p * 20 : p * 20 + 20, :] = cyc_g[p // NY % 4 // 2, p // NY % 2, p // NY // 4, p % NY][:20, :].astype(F32)

    def mask_w(c, _):
        rows = pl.ds(pl.multiple_of(c * 128, 128), 128)
        for k in range(5):
            cols = slice(k * 128, (k + 1) * 128)
            keep = irr_c[rows, :] == irow_ref[:, cols]
            w_b[rows, cols] = jnp.where(keep, w_stage[rows, cols], 0.0).astype(BF16)
        return 0

    lax.fori_loop(0, 5, mask_w, 0)

    def dress(b, _):
        await_bytes(amp_v.at[pl.ds(0, 16)], amp_sem.at[b])

        def quad(q, _):
            ij = b * 16 + q * 8
            x = amp_v[pl.ds(ij, 8)].reshape(512, 640)
            v = jnp.dot(x, w_b[...], preferred_element_type=F32) + x.astype(F32)
            for e in range(8):
                label = pirr[ij + e]
                at = pl.ds((q * 8 + e) * 65, 64)
                for k in range(5):
                    cols = slice(k * 128, (k + 1) * 128)
                    y_stage[k, at, :] = jnp.where(irr_x[:, cols] == label, v[e * 64 : (e + 1) * 64, cols], 0.0)
            return 0

        lax.fori_loop(0, 2, quad, 0)

        def turn(c, _):
            at = pl.ds(pl.multiple_of(b * 16, 16), 16)
            got = [y_stage[k, pl.ds(c * 8 + i, 16, stride=65), :].astype(BF16) for i in range(8) for k in range(5)]
            for i in range(40):
                dressed[c * 40 + i, at, :] = got[i]
            return 0

        lax.fori_loop(0, 8, turn, 0)
        return 0

    lax.fori_loop(0, 2, dress, 0)
    forward(0)
    lax.fori_loop(2, 4, dress, 0)

    def order(delta):
        def one(yy, _):
            first = (wrap(z + delta, NZ) * NY + yy) * 10
            for s in range(10):
                d_send[delta % 8, yy, :, s * 128 : (s + 1) * 128] = dressed[towners[r, first + s]]
            return 0

        lax.fori_loop(0, NY, one, 0)

    mine = pl.ds(pl.multiple_of(y * 64, 64), 64)

    def send(delta):
        order(delta)
        buf = d_send.at[delta % 8]
        if delta in FAR:
            to, sem = far.at[FAR[delta], mine], x_recv.at[FAR[delta]]
        else:
            to, sem = recv_f.at[NEAR[delta], mine], a_recv.at[NEAR[delta]]
        local(buf.at[y], to, sem)
        for k in (2, 1, 3):
            yy = wrap(y + k, NY)
            remote(buf.at[yy], to, a_send.at[delta % 8], sem, dev(z, yy, r))

    def sent(delta):
        await_bytes(d_send.at[0, pl.ds(0, NY - 1)], a_send.at[delta % 8])

    def go_on(delta):
        at = FAR[delta]
        await_bytes(far.at[at], x_recv.at[at])
        if delta == 4:
            remote(far.at[at, pl.ds(0, 128)], recv_h.at[0], x_send, a_recv.at[7], dev(z + 2, y, r))
            remote(far.at[at, pl.ds(128, 128)], recv_h.at[1], x_send, a_recv.at[8], dev(z - 2, y, r))
        else:
            remote(far.at[at], recv_f.at[3 + at], x_send, a_recv.at[3 + at], dev(z + 1 - 2 * at, y, r))

    for delta in WAY[:WINDOW]:
        send(delta)
    forward(1)

    def multiply(x, w, o):
        def cols(n, _):
            at = pl.ds(pl.multiple_of(n * 256, 256), 256)
            o[:, at] = jnp.dot(x[...], w[:, at], preferred_element_type=F32).astype(BF16)
            return 0

        lax.fori_loop(0, 2, cols, 0)

    def scatter(o, rr, n, sem):
        def piece(q):
            return o.at[pl.ds(pl.multiple_of(q * n, n), n)]

        for k in (4, 3, 5, 2, 6, 1, 7):
            q = wrap(r + k, NR)
            remote(piece(q), rr.at[r], r_send, sem, dev(z, y, q))
        local(piece(r), rr.at[r], sem)

    def reduce(item):
        if item < 7:
            (o, s), rr, fb, n = FULL[item], rr_f.at[item], fb_f.at[item], 32
            row = r * 32
        else:
            (o, s), rr, fb, n = HALF[item - 7], rr_h.at[item - 7], fb_h.at[item - 7], 16
            row = r * 16 + (item - 7) * 128
        await_bytes(rr, r_recv.at[item])
        total = rr[0].astype(F32)
        for q in range(1, NR):
            total = total + rr[q].astype(F32)
        fb[...] = total.astype(BF16)
        rows = outb.at[pl.ds(pl.multiple_of(row, 16), n)]
        level = wrap(z + s, NZ)
        if item == 0:

            @pl.when(level == r)
            def _():
                local(fb, rows, f_recv)

            @pl.when(level != r)
            def _():
                remote(fb, rows, f_send.at[0], f_recv, dev(z + o, y, level))
        else:
            remote(fb, rows, f_send.at[1], f_recv, dev(z + o, y, level))

    ready = {2}

    def item_step(item):
        if item < 7:
            o, x, ob, rr, n = FULL[item][0], recv_f.at[item], ob_f.at[item], rr_f.at[item], 32
        else:
            o, x, ob, rr, n = HALF[item - 7][0], recv_h.at[item - 7], ob_h.at[item - 7], rr_h.at[item - 7], 16
        if item == 0:
            await_bytes(wbuf.at[2], own_sem)
        if o in (2, -2) and o + 2 not in ready:
            ready.add(o + 2)
            for h in range(2):
                await_bytes(wbuf.at[o + 2, pl.ds(h * 640, 640)], w_recv.at[o + 2, h])
        await_bytes(x, a_recv.at[item])
        multiply(x, wbuf.at[o + 2], ob)
        scatter(ob, rr, n, r_recv.at[item])

    pending = []
    for i, delta in enumerate(WAY):
        if i + WINDOW < 8:
            sent(delta)
            send(WAY[i + WINDOW])
        if delta in FAR:
            go_on(delta)
            continue
        for item in TODO[delta]:
            item_step(item)
            if pending and item < 7:
                reduce(pending.pop(0))
            pending.append(item)
    for item in pending:
        reduce(item)

    diag64 = lax.broadcasted_iota(I32, (64, 128), 0) == lax.broadcasted_iota(I32, (64, 128), 1)
    await_bytes(outb, f_recv)
    for j in range(4):
        t = ltiles[j, pair]
        la, bb = oirr[lax.div(t, 5)], lax.rem(t, 5)
        lab = jnp.zeros((1, 128), I32)
        for k in range(5):
            lab = lab + jnp.where(bb == k, irow_ref[:, k * 128 : (k + 1) * 128], 0)
        lab = jnp.bitwise_xor(lab, la).astype(F32)
        for yy in range(NY):
            rowl = cyc_g[side, core, lax.div(r, 4), yy][20:21, 0:128].astype(F32)
            col = jnp.sum(jnp.where(diag64, jnp.broadcast_to(rowl, (64, 128)), 0.0), axis=1, keepdims=True)
            keep = jnp.broadcast_to(col, (64, 128)) == lab
            got = outb[yy * 64 : (yy + 1) * 64, j * 128 : (j + 1) * 128].astype(F32)
            out_ref[yy * 64 : (yy + 1) * 64, j * 128 : (j + 1) * 128] = jnp.where(keep, got, 0.0).astype(BF16)

    @pl.when(sends)
    def _():
        await_bytes(cyc_g.at[0, 0, 0], c_send.at[0])
        await_bytes(cyc_g.at[0, 0, 0, pl.ds(0, 3)], c_send.at[0])

    await_bytes(cyc_g.at[0, 0, :, pl.ds(0, NY - 1)], c_send.at[1])
    await_bytes(cyc_g.at[0, 0], c_send.at[2])
    await_bytes(cyc_g.at[:, 0], c_send.at[3])
    await_bytes(wbuf.at[pl.ds(0, 4)], w_send)
    for delta in WAY[8 - WINDOW :]:
        sent(delta)
    await_bytes(far, x_send)
    await_bytes(rr_f.at[:, pl.ds(0, NR - 1)], r_send)
    await_bytes(rr_h.at[:, pl.ds(0, NR - 1)], r_send)

    @pl.when(z != r)
    def _():
        await_bytes(fb_f.at[0], f_send.at[0])

    await_bytes(fb_f.at[pl.ds(0, 6)], f_send.at[1])
    await_bytes(fb_h, f_send.at[1])


def shards(amplitudes, cycle_integrals, ladder_integrals, orbital_irrep, pair_irrep, tile_owners, ladder_tiles):
    hbm = pl.BlockSpec(memory_space=pltpu.MemorySpace.HBM)
    vmem = pl.BlockSpec(memory_space=pltpu.MemorySpace.VMEM)
    smem = pl.BlockSpec(memory_space=pltpu.MemorySpace.SMEM)
    dma = pltpu.SemaphoreType.DMA
    out = pl.pallas_call(
        kernel,
        out_shape=jax.ShapeDtypeStruct((256, 512), BF16),
        in_specs=[hbm, vmem, hbm, vmem, vmem, smem, smem, smem, smem],
        out_specs=vmem,
        scratch_shapes=[
            pltpu.VMEM((64, 64, 640), BF16),
            pltpu.VMEM((24, 640), BF16),
            pltpu.VMEM((2, 2, 2, 4, 24, 640), BF16),
            pltpu.VMEM((640, 640), F32),
            pltpu.VMEM((640, 640), BF16),
            pltpu.VMEM((1, 640), I32),
            pltpu.VMEM((64, 640), I32),
            pltpu.VMEM((640, 128), I32),
            pltpu.VMEM((5, 1152, 128), F32),
            pltpu.VMEM((320, 64, 128), BF16),
            pltpu.VMEM((8, 4, 64, 1280), BF16),
            pltpu.VMEM((7, 256, 1280), BF16),
            pltpu.VMEM((2, 128, 1280), BF16),
            pltpu.VMEM((3, 256, 1280), BF16),
            pltpu.VMEM((5, 1280, 512), BF16),
            pltpu.VMEM((7, 256, 512), BF16),
            pltpu.VMEM((2, 128, 512), BF16),
            pltpu.VMEM((7, 8, 32, 512), BF16),
            pltpu.VMEM((2, 8, 16, 512), BF16),
            pltpu.VMEM((7, 32, 512), BF16),
            pltpu.VMEM((2, 16, 512), BF16),
            pltpu.VMEM((256, 512), BF16),
            dma((4,)),
            dma,
            dma((4,)),
            dma((4,)),
            dma,
            dma((5, 2)),
            dma((8,)),
            dma((9,)),
            dma,
            dma((3,)),
            dma,
            dma((9,)),
            dma((2,)),
            dma,
        ],
        compiler_params=pltpu.CompilerParams(
            collective_id=0, has_side_effects=True, vmem_limit_bytes=56 << 20
        ),
        name="ladder",
    )(
        amplitudes,
        cycle_integrals,
        ladder_integrals.reshape(1280, 512),
        orbital_irrep,
        pair_irrep,
        tile_owners,
        ladder_tiles.T,
        orbital_irrep,
        pair_irrep,
    )
    return out[None]


def solution(mesh):
    return jax.shard_map(
        shards,
        mesh=mesh,
        in_specs=(
            P("pair", "red", None),
            P("pair", None),
            P("pair", "red", None, None),
            P(),
            P("pair"),
            P(),
            P(),
        ),
        out_specs=P("pair", "red", None),
        check_vma=False,
    )
```

```python
import jax
import jax.numpy as jnp
from jax import lax
from jax.experimental import pallas as pl
from jax.experimental.pallas import tpu as pltpu
from jax.sharding import PartitionSpec as P

NZ, NY, NR = 8, 4, 8
F32, BF16, I32 = jnp.float32, jnp.bfloat16, jnp.int32
FULL = ((0, 0), (1, 0), (-1, 0), (2, -1), (-2, 1), (2, 0), (-2, 0))
HALF = ((2, -2), (-2, 2))
WAY = (0, 3, -3, 4, 1, -1, 2, -2)
NEAR = {0: 0, 1: 1, -1: 2, 2: 5, -2: 6}
FAR = {3: 0, -3: 1, 4: 2}
TODO = {0: (0,), 1: (1,), -1: (2,), 2: (3, 4, 5), -2: (6,)}
WINDOW = 3


def wrap(v, n):
    return lax.rem(v + n, n)


def kernel(
    amp_hbm, cyc_hbm, lad_hbm, to_hbm, lt_hbm, oi_hbm, pi_hbm,
    out_hbm,
    cyc_in, orow, prow, towners, ltiles, oirr, pirr, out_ref,
    row_lab, col_lab, amp_v, cyc_ref, cyc_g, w_stage, w_b, irow_ref, irr_x, irr_c, y_stage, dressed, d_send,
    recv_f, recv_h, far, wbuf, ob_f, ob_h, rr_f, rr_h, fb_f, fb_h, outb,
    in_sem, out_sem, amp_sem, own_sem, c_send, c_recv, w_send, w_recv, a_send, a_recv,
    x_send, x_recv, r_send, r_recv, f_send, f_recv,
):
    pair = lax.axis_index("pair")
    r = lax.axis_index("red")
    z, y = lax.div(pair, NY), lax.rem(pair, NY)

    def dev(zz, yy, rr):
        return (wrap(zz, NZ) * NY + wrap(yy, NY), wrap(rr, NR))

    def remote(src, dst, ssem, rsem, where):
        pltpu.make_async_remote_copy(
            src_ref=src, dst_ref=dst, send_sem=ssem, recv_sem=rsem,
            device_id=where, device_id_type=pl.DeviceIdType.MESH,
        ).start()

    def local(src, dst, sem):
        pltpu.make_async_copy(src, dst, sem).start()

    def await_bytes(ref, sem):
        pltpu.make_async_copy(ref, ref, sem).wait()

    bar = pltpu.get_barrier_semaphore()

    def greet(where):
        pl.semaphore_signal(bar, inc=1, device_id=where, device_id_type=pl.DeviceIdType.MESH)

    for k in (1, 7, 2, 6, 3, 5, 4):
        greet(dev(z + k, y, r))
    for k in range(1, NR):
        greet(dev(z, y, r + k))
    for k in range(1, NY):
        greet(dev(z, y + k, r))
    offset = lax.rem(z + NZ - r, NZ)
    for o, s in FULL[1:] + HALF:
        greet(dev(z + o, y, z + s))
    for k in range(1, NR):
        greet(dev(r + jnp.where(offset == 3, 1, jnp.where(offset == 5, -1, jnp.where(offset == 4, 2, 0))), y, r + k))

    @pl.when(offset != 0)
    def _():
        greet(dev(z, y, z))
        greet(dev(r + jnp.where(offset == 3, 1, jnp.where(offset == 5, -1, jnp.where(offset == 4, 2, 0))), y, r))

    @pl.when(offset == 4)
    def _():
        for k in range(NR):
            greet(dev(r - 2, y, k))

    small = (
        (cyc_hbm, cyc_in), (oi_hbm, orow), (pi_hbm, prow), (to_hbm, towners),
        (lt_hbm, ltiles), (oi_hbm, oirr), (pi_hbm, pirr),
    )
    for i, (src, dst) in enumerate(small):
        local(src, dst, in_sem.at[i])
    for b in range(4):
        rows = pl.ds(b * 16, 16)
        local(amp_hbm.at[rows], amp_v.at[rows], amp_sem.at[b])
    local(lad_hbm, wbuf.at[2], own_sem)

    for i, (src, dst) in enumerate(small):
        pltpu.make_async_copy(src, dst, in_sem.at[i]).wait()
    for k in range(5):
        irow_ref[:, k * 128 : (k + 1) * 128] = orow[pl.ds(k * 128, 128)].reshape(1, 128)
    cyc_ref[0:20, :] = cyc_in[...]
    cyc_ref[20:24, :] = jnp.zeros((4, 640), BF16)
    cyc_ref[20:24, 0:64] = jnp.broadcast_to(prow[...].reshape(1, 64), (4, 64)).astype(BF16)
    diag = lax.broadcasted_iota(I32, (128, 128), 0) == lax.broadcasted_iota(I32, (128, 128), 1)
    for k in range(5):
        lab = jnp.broadcast_to(irow_ref[:, k * 128 : (k + 1) * 128], (128, 128))
        col = jnp.sum(jnp.where(diag, lab, 0), axis=1, keepdims=True)
        irr_c[k * 128 : (k + 1) * 128, :] = jnp.broadcast_to(col, (128, 128))
    slab = irr_c[pl.ds(pl.multiple_of(r * 64, 64), 64), :]
    for k in range(5):
        irr_x[:, k * 128 : (k + 1) * 128] = jnp.bitwise_xor(slab, irow_ref[:, k * 128 : (k + 1) * 128])

    pl.semaphore_wait(bar, 34 + jnp.where(offset == 4, 8, 0) - jnp.where(offset == 0, 2, 0))

    side, core = lax.rem(lax.div(r, 2), 2), lax.rem(r, 2)
    sends = lax.rem(z, 4) == lax.rem(r, 4)

    @pl.when(sends)
    def _():
        to = cyc_g.at[side, core, lax.div(z, 4), y]
        local(cyc_ref, to, c_recv.at[0])
        for k in (4, 3, 5, 2, 6, 1, 7):
            remote(cyc_ref, to, c_send.at[0], c_recv.at[0], dev(z + k, y, r))

    for h in range(2):
        rows = pl.ds(h * 640, 640)
        remote(lad_hbm.at[rows], wbuf.at[1, rows], w_send, w_recv.at[1, h], dev(z + 1, y, r))
        remote(lad_hbm.at[rows], wbuf.at[3, rows], w_send, w_recv.at[3, h], dev(z - 1, y, r))

    part = cyc_g.at[side, core, :, y]
    await_bytes(part, c_recv.at[0])
    for k in (2, 1, 3):
        remote(part, part, c_send.at[1], c_recv.at[1], dev(z, y + k, r))
    await_bytes(cyc_g.at[0, 0, :, pl.ds(0, NY - 1)], c_recv.at[1])
    for h, dr in ((0, -2), (1, 2)):
        part = cyc_g.at[side, core, h]
        remote(part, part, c_send.at[2], c_recv.at[2], dev(z, y, r + dr))
    partner = dev(z, y, r + 1 - 2 * core)
    part = cyc_g.at[side, core]
    remote(part, part, c_send.at[3], c_recv.at[3], partner)
    part = cyc_g.at[1 - side, core]
    await_bytes(part, c_recv.at[2])
    remote(part, part, c_send.at[3], c_recv.at[3], partner)
    await_bytes(cyc_g.at[:, 0], c_recv.at[3])

    def forward(h):
        rows = pl.ds(h * 640, 640)
        for a, b, dz in ((1, 0, 1), (3, 4, -1)):
            await_bytes(wbuf.at[a, rows], w_recv.at[a, h])
            remote(wbuf.at[a, rows], wbuf.at[b, rows], w_send, w_recv.at[b, h], dev(z + dz, y, r))

    for p in range(NZ * NY):
        w_stage[p * 20 : p * 20 + 20, :] = cyc_g[p // NY % 4 // 2, p // NY % 2, p // NY // 4, p % NY][:20, :].astype(F32)

    def mask_w(c, _):
        rows = pl.ds(pl.multiple_of(c * 128, 128), 128)
        for k in range(5):
            cols = slice(k * 128, (k + 1) * 128)
            keep = irr_c[rows, :] == irow_ref[:, cols]
            w_b[rows, cols] = jnp.where(keep, w_stage[rows, cols], 0.0).astype(BF16)
        return 0

    lax.fori_loop(0, 5, mask_w, 0)

    def dress(b, _):
        await_bytes(amp_v.at[pl.ds(0, 16)], amp_sem.at[b])

        def quad(q, _):
            ij = b * 16 + q * 8
            x = amp_v[pl.ds(ij, 8)].reshape(512, 640)
            v = jnp.dot(x, w_b[...], preferred_element_type=F32) + x.astype(F32)
            for e in range(8):
                label = pirr[ij + e]
                at = pl.ds((q * 8 + e) * 65, 64)
                for k in range(5):
                    cols = slice(k * 128, (k + 1) * 128)
                    y_stage[k, at, :] = jnp.where(irr_x[:, cols] == label, v[e * 64 : (e + 1) * 64, cols], 0.0)
            return 0

        lax.fori_loop(0, 2, quad, 0)

        def turn(c, _):
            at = pl.ds(pl.multiple_of(b * 16, 16), 16)
            got = [y_stage[k, pl.ds(c * 8 + i, 16, stride=65), :].astype(BF16) for i in range(8) for k in range(5)]
            for i in range(40):
                dressed[c * 40 + i, at, :] = got[i]
            return 0

        lax.fori_loop(0, 8, turn, 0)
        return 0

    lax.fori_loop(0, 2, dress, 0)
    forward(0)
    lax.fori_loop(2, 4, dress, 0)

    def order(delta):
        def one(yy, _):
            first = (wrap(z + delta, NZ) * NY + yy) * 10
            for s in range(10):
                d_send[delta % 8, yy, :, s * 128 : (s + 1) * 128] = dressed[towners[r, first + s]]
            return 0

        lax.fori_loop(0, NY, one, 0)

    mine = pl.ds(pl.multiple_of(y * 64, 64), 64)

    def send(delta):
        order(delta)
        buf = d_send.at[delta % 8]
        if delta in FAR:
            to, sem = far.at[FAR[delta], mine], x_recv.at[FAR[delta]]
        else:
            to, sem = recv_f.at[NEAR[delta], mine], a_recv.at[NEAR[delta]]
        local(buf.at[y], to, sem)
        for k in (2, 1, 3):
            yy = wrap(y + k, NY)
            remote(buf.at[yy], to, a_send.at[delta % 8], sem, dev(z, yy, r))

    def sent(delta):
        await_bytes(d_send.at[0, pl.ds(0, NY - 1)], a_send.at[delta % 8])

    def go_on(delta):
        at = FAR[delta]
        await_bytes(far.at[at], x_recv.at[at])
        if delta == 4:
            for part in range(2):
                rows = pl.ds(part * 64, 64)
                remote(far.at[at, rows], recv_h.at[0, rows], x_send, a_recv.at[7 + part], dev(z + 2, y, r))
                low = pl.ds(128 + part * 64, 64)
                remote(far.at[at, low], recv_h.at[1, rows], x_send, a_recv.at[9 + part], dev(z - 2, y, r))
        else:
            remote(far.at[at], recv_f.at[3 + at], x_send, a_recv.at[3 + at], dev(z + 1 - 2 * at, y, r))

    for delta in WAY[:WINDOW]:
        send(delta)
    forward(1)

    diag64 = lax.broadcasted_iota(I32, (64, 128), 0) == lax.broadcasted_iota(I32, (64, 128), 1)
    for yy in range(NY):
        rowl = cyc_g[side, core, lax.div(r, 4), yy][20:21, 0:128].astype(F32)
        col = jnp.sum(jnp.where(diag64, jnp.broadcast_to(rowl, (64, 128)), 0.0), axis=1, keepdims=True)
        row_lab[yy * 64 : (yy + 1) * 64, :] = jnp.broadcast_to(col, (64, 128))
    for j in range(4):
        t = ltiles[j, pair]
        la, bb = oirr[lax.div(t, 5)], lax.rem(t, 5)
        lab = jnp.zeros((1, 128), I32)
        for k in range(5):
            lab = lab + jnp.where(bb == k, irow_ref[:, k * 128 : (k + 1) * 128], 0)
        col_lab[j : j + 1, :] = jnp.bitwise_xor(lab, la).astype(F32)

    def multiply(x, w, o):
        def cols(n, _):
            at = pl.ds(pl.multiple_of(n * 256, 256), 256)
            o[:, at] = jnp.dot(x[...], w[:, at], preferred_element_type=F32).astype(BF16)
            return 0

        lax.fori_loop(0, 2, cols, 0)

    def scatter(o, rr, n, sem):
        def piece(q):
            return o.at[pl.ds(pl.multiple_of(q * n, n), n)]

        for k in (4, 3, 5, 2, 6, 1, 7):
            q = wrap(r + k, NR)
            remote(piece(q), rr.at[r], r_send, sem, dev(z, y, q))
        local(piece(r), rr.at[r], sem)

    def reduce(item):
        if item < 7:
            (o, s), rr, fb, n = FULL[item], rr_f.at[item], fb_f.at[item], 32
            row = r * 32
        else:
            (o, s), rr, fb, n = HALF[item - 7], rr_h.at[item - 7], fb_h.at[item - 7], 16
            row = r * 16 + (item - 7) * 128
        await_bytes(rr, r_recv.at[item])
        total = rr[0].astype(F32)
        for q in range(1, NR):
            total = total + rr[q].astype(F32)
        fb[...] = total.astype(BF16)
        rows = outb.at[pl.ds(pl.multiple_of(row, 16), n)]
        level = wrap(z + s, NZ)
        if item == 0:

            @pl.when(level == r)
            def _():
                local(fb, rows, f_recv)

            @pl.when(level != r)
            def _():
                remote(fb, rows, f_send.at[0], f_recv, dev(z + o, y, level))
        else:
            remote(fb, rows, f_send.at[1], f_recv, dev(z + o, y, level))

    ready = {2}

    def half_step(item, part):
        h, rows = item - 7, pl.ds(part * 64, 64)
        await_bytes(recv_h.at[h, rows], a_recv.at[7 + 2 * h + part])
        multiply(recv_h.at[h, rows], wbuf.at[HALF[h][0] + 2], ob_h.at[h, rows])

        def piece(q):
            return ob_h.at[h, pl.ds(pl.multiple_of(q * 16, 16), 16)]

        for k in (2, 1, 3):
            q = part * 4 + lax.rem(r + k, 4)
            remote(piece(q), rr_h.at[h, r], r_send, r_recv.at[item], dev(z, y, q))
        q = part * 4 + lax.rem(r, 4)

        @pl.when(q == r)
        def _():
            local(piece(r), rr_h.at[h, r], r_recv.at[item])

        @pl.when(q != r)
        def _():
            remote(piece(q), rr_h.at[h, r], r_send, r_recv.at[item], dev(z, y, q))

    def item_step(item):
        o, x, ob, rr, n = FULL[item][0], recv_f.at[item], ob_f.at[item], rr_f.at[item], 32
        if item == 0:
            await_bytes(wbuf.at[2], own_sem)
        if o in (2, -2) and o + 2 not in ready:
            ready.add(o + 2)
            for h in range(2):
                await_bytes(wbuf.at[o + 2, pl.ds(h * 640, 640)], w_recv.at[o + 2, h])
        await_bytes(x, a_recv.at[item])
        multiply(x, wbuf.at[o + 2], ob)
        scatter(ob, rr, n, r_recv.at[item])

    pending = []
    for i, delta in enumerate(WAY):
        if i + WINDOW < 8:
            sent(delta)
            send(WAY[i + WINDOW])
        if delta in FAR:
            go_on(delta)
            continue
        for item in TODO[delta]:
            item_step(item)
            if len(pending) > 1:
                reduce(pending.pop(0))
            pending.append(item)
    for part in range(2):
        for item in (7, 8):
            half_step(item, part)
    for item in (*pending, 7, 8):
        reduce(item)

    await_bytes(outb, f_recv)
    for yy in range(NY):
        for j in range(4):
            got = outb[yy * 64 : (yy + 1) * 64, j * 128 : (j + 1) * 128].astype(F32)
            keep = row_lab[yy * 64 : (yy + 1) * 64, :] == col_lab[j : j + 1, :]
            out_ref[yy * 64 : (yy + 1) * 64, j * 128 : (j + 1) * 128] = jnp.where(keep, got, 0.0).astype(BF16)
    local(out_ref, out_hbm, out_sem)

    @pl.when(sends)
    def _():
        await_bytes(cyc_g.at[0, 0, 0], c_send.at[0])
        await_bytes(cyc_g.at[0, 0, 0, pl.ds(0, 3)], c_send.at[0])

    await_bytes(cyc_g.at[0, 0, :, pl.ds(0, NY - 1)], c_send.at[1])
    await_bytes(cyc_g.at[0, 0], c_send.at[2])
    await_bytes(cyc_g.at[:, 0], c_send.at[3])
    await_bytes(wbuf.at[pl.ds(0, 4)], w_send)
    for delta in WAY[8 - WINDOW :]:
        sent(delta)
    await_bytes(far, x_send)
    await_bytes(rr_f.at[:, pl.ds(0, NR - 1)], r_send)
    await_bytes(rr_h.at[:, pl.ds(0, NR - 1)], r_send)

    @pl.when(z != r)
    def _():
        await_bytes(fb_f.at[0], f_send.at[0])

    await_bytes(fb_f.at[pl.ds(0, 6)], f_send.at[1])
    await_bytes(fb_h, f_send.at[1])
    pltpu.make_async_copy(out_ref, out_hbm, out_sem).wait()


def shards(amplitudes, cycle_integrals, ladder_integrals, orbital_irrep, pair_irrep, tile_owners, ladder_tiles):
    hbm = pl.BlockSpec(memory_space=pltpu.MemorySpace.HBM)
    dma = pltpu.SemaphoreType.DMA
    out = pl.pallas_call(
        kernel,
        out_shape=jax.ShapeDtypeStruct((256, 512), BF16),
        in_specs=[hbm] * 7,
        out_specs=hbm,
        scratch_shapes=[
            pltpu.VMEM((20, 640), BF16),
            pltpu.VMEM((640,), I32),
            pltpu.VMEM((64,), I32),
            pltpu.SMEM((8, 320), I32),
            pltpu.SMEM((4, 32), I32),
            pltpu.SMEM((640,), I32),
            pltpu.SMEM((64,), I32),
            pltpu.VMEM((256, 512), BF16),
            pltpu.VMEM((256, 128), F32),
            pltpu.VMEM((4, 128), F32),
            pltpu.VMEM((64, 64, 640), BF16),
            pltpu.VMEM((24, 640), BF16),
            pltpu.VMEM((2, 2, 2, 4, 24, 640), BF16),
            pltpu.VMEM((640, 640), F32),
            pltpu.VMEM((640, 640), BF16),
            pltpu.VMEM((1, 640), I32),
            pltpu.VMEM((64, 640), I32),
            pltpu.VMEM((640, 128), I32),
            pltpu.VMEM((5, 1152, 128), F32),
            pltpu.VMEM((320, 64, 128), BF16),
            pltpu.VMEM((8, 4, 64, 1280), BF16),
            pltpu.VMEM((7, 256, 1280), BF16),
            pltpu.VMEM((2, 128, 1280), BF16),
            pltpu.VMEM((3, 256, 1280), BF16),
            pltpu.VMEM((5, 1280, 512), BF16),
            pltpu.VMEM((7, 256, 512), BF16),
            pltpu.VMEM((2, 128, 512), BF16),
            pltpu.VMEM((7, 8, 32, 512), BF16),
            pltpu.VMEM((2, 8, 16, 512), BF16),
            pltpu.VMEM((7, 32, 512), BF16),
            pltpu.VMEM((2, 16, 512), BF16),
            pltpu.VMEM((256, 512), BF16),
            dma((7,)),
            dma,
            dma((4,)),
            dma,
            dma((4,)),
            dma((4,)),
            dma,
            dma((5, 2)),
            dma((8,)),
            dma((11,)),
            dma,
            dma((3,)),
            dma,
            dma((9,)),
            dma((2,)),
            dma,
        ],
        compiler_params=pltpu.CompilerParams(
            collective_id=0, has_side_effects=True, vmem_limit_bytes=56 << 20
        ),
        name="ladder",
    )(
        amplitudes,
        cycle_integrals,
        ladder_integrals.reshape(1280, 512),
        tile_owners,
        ladder_tiles.T,
        orbital_irrep,
        pair_irrep,
    )
    return out[None]


def solution(mesh):
    return jax.shard_map(
        shards,
        mesh=mesh,
        in_specs=(
            P("pair", "red", None),
            P("pair", None),
            P("pair", "red", None, None),
            P(),
            P("pair"),
            P(),
            P(),
        ),
        out_specs=P("pair", "red", None),
        check_vma=False,
    )
```

```python
import jax
import jax.numpy as jnp
from jax import lax
from jax.experimental import pallas as pl
from jax.experimental.pallas import tpu as pltpu
from jax.sharding import PartitionSpec as P

NZ, NY, NR = 8, 4, 8
F32, BF16, I32 = jnp.float32, jnp.bfloat16, jnp.int32
FULL = ((0, 0), (1, 0), (-1, 0), (2, -1), (-2, 1), (2, 0), (-2, 0))
HALF = ((2, -2), (-2, 2))
WAY = (0, 3, -3, 4, 1, -1, 2, -2)
NEAR = {0: 0, 1: 1, -1: 2, 2: 5, -2: 6}
FAR = {3: 0, -3: 1, 4: 2}
TODO = {0: (0,), 1: (1,), -1: (2,), 2: (3, 4, 5), -2: (6,)}
WINDOW = 3


def wrap(v, n):
    return lax.rem(v + n, n)


def kernel(
    amp_hbm, cyc_hbm, lad_hbm, to_hbm, lt_hbm, oi_hbm, pi_hbm,
    out_hbm, keep_hbm,
    cyc_in, orow, prow, towners, ltiles, oirr, pirr, keep,
    amp_v, cyc_ref, cyc_g, w_stage, w_b, irow_ref, irr_x, irr_c, y_stage, dressed, d_send,
    recv_f, recv_h, far, wbuf, ob_f, ob_h, rr_f, rr_h, fb_f, fb_h,
    in_sem, out_sem, amp_sem, own_sem, c_send, c_recv, w_send, w_recv, a_send, a_recv,
    x_send, x_recv, r_send, r_recv, f_send, f_recv,
):
    pair = lax.axis_index("pair")
    r = lax.axis_index("red")
    z, y = lax.div(pair, NY), lax.rem(pair, NY)

    def dev(zz, yy, rr):
        return (wrap(zz, NZ) * NY + wrap(yy, NY), wrap(rr, NR))

    def remote(src, dst, ssem, rsem, where):
        pltpu.make_async_remote_copy(
            src_ref=src, dst_ref=dst, send_sem=ssem, recv_sem=rsem,
            device_id=where, device_id_type=pl.DeviceIdType.MESH,
        ).start()

    def local(src, dst, sem):
        pltpu.make_async_copy(src, dst, sem).start()

    def await_bytes(ref, sem):
        pltpu.make_async_copy(ref, ref, sem).wait()

    bar = pltpu.get_barrier_semaphore()

    def greet(where):
        pl.semaphore_signal(bar, inc=1, device_id=where, device_id_type=pl.DeviceIdType.MESH)

    for k in (1, 7, 2, 6, 3, 5, 4):
        greet(dev(z + k, y, r))
    for k in range(1, NR):
        greet(dev(z, y, r + k))
    for k in range(1, NY):
        greet(dev(z, y + k, r))
    small = (
        (cyc_hbm, cyc_in), (oi_hbm, orow), (pi_hbm, prow), (to_hbm, towners),
        (lt_hbm, ltiles), (oi_hbm, oirr), (pi_hbm, pirr),
    )
    for i, (src, dst) in enumerate(small):
        local(src, dst, in_sem.at[i])
    for b in range(4):
        rows = pl.ds(b * 16, 16)
        local(amp_hbm.at[rows], amp_v.at[rows], amp_sem.at[b])
    local(lad_hbm, wbuf.at[2], own_sem)

    for i, (src, dst) in enumerate(small):
        pltpu.make_async_copy(src, dst, in_sem.at[i]).wait()
    for k in range(5):
        irow_ref[:, k * 128 : (k + 1) * 128] = orow[pl.ds(k * 128, 128)].reshape(1, 128)
    cyc_ref[0:20, :] = cyc_in[...]
    cyc_ref[20:24, :] = jnp.zeros((4, 640), BF16)
    cyc_ref[20:24, 0:64] = jnp.broadcast_to(prow[...].reshape(1, 64), (4, 64)).astype(BF16)
    diag = lax.broadcasted_iota(I32, (128, 128), 0) == lax.broadcasted_iota(I32, (128, 128), 1)
    for k in range(5):
        lab = jnp.broadcast_to(irow_ref[:, k * 128 : (k + 1) * 128], (128, 128))
        col = jnp.sum(jnp.where(diag, lab, 0), axis=1, keepdims=True)
        irr_c[k * 128 : (k + 1) * 128, :] = jnp.broadcast_to(col, (128, 128))
    slab = irr_c[pl.ds(pl.multiple_of(r * 64, 64), 64), :]
    for k in range(5):
        irr_x[:, k * 128 : (k + 1) * 128] = jnp.bitwise_xor(slab, irow_ref[:, k * 128 : (k + 1) * 128])

    pl.semaphore_wait(bar, 2 * (NZ - 1) + NY - 1)

    side, core = lax.rem(lax.div(r, 2), 2), lax.rem(r, 2)
    sends = lax.rem(z, 4) == lax.rem(r, 4)

    @pl.when(sends)
    def _():
        to = cyc_g.at[side, core, lax.div(z, 4), y]
        local(cyc_ref, to, c_recv.at[0])
        for k in (4, 3, 5, 2, 6, 1, 7):
            remote(cyc_ref, to, c_send.at[0], c_recv.at[0], dev(z + k, y, r))

    for h in range(2):
        rows = pl.ds(h * 640, 640)
        remote(lad_hbm.at[rows], wbuf.at[1, rows], w_send, w_recv.at[1, h], dev(z + 1, y, r))
        remote(lad_hbm.at[rows], wbuf.at[3, rows], w_send, w_recv.at[3, h], dev(z - 1, y, r))

    part = cyc_g.at[side, core, :, y]
    await_bytes(part, c_recv.at[0])
    for k in (2, 1, 3):
        remote(part, part, c_send.at[1], c_recv.at[1], dev(z, y + k, r))
    await_bytes(cyc_g.at[0, 0, :, pl.ds(0, NY - 1)], c_recv.at[1])
    for h, dr in ((0, -2), (1, 2)):
        part = cyc_g.at[side, core, h]
        remote(part, part, c_send.at[2], c_recv.at[2], dev(z, y, r + dr))
    partner = dev(z, y, r + 1 - 2 * core)
    part = cyc_g.at[side, core]
    remote(part, part, c_send.at[3], c_recv.at[3], partner)
    part = cyc_g.at[1 - side, core]
    await_bytes(part, c_recv.at[2])
    remote(part, part, c_send.at[3], c_recv.at[3], partner)
    await_bytes(cyc_g.at[:, 0], c_recv.at[3])

    def forward(h):
        rows = pl.ds(h * 640, 640)
        for a, b, dz in ((1, 0, 1), (3, 4, -1)):
            await_bytes(wbuf.at[a, rows], w_recv.at[a, h])
            remote(wbuf.at[a, rows], wbuf.at[b, rows], w_send, w_recv.at[b, h], dev(z + dz, y, r))

    for p in range(NZ * NY):
        w_stage[p * 20 : p * 20 + 20, :] = cyc_g[p // NY % 4 // 2, p // NY % 2, p // NY // 4, p % NY][:20, :].astype(F32)

    def mask_w(c, _):
        rows = pl.ds(pl.multiple_of(c * 128, 128), 128)
        for k in range(5):
            cols = slice(k * 128, (k + 1) * 128)
            keep = irr_c[rows, :] == irow_ref[:, cols]
            w_b[rows, cols] = jnp.where(keep, w_stage[rows, cols], 0.0).astype(BF16)
        return 0

    lax.fori_loop(0, 5, mask_w, 0)

    def dress(b, _):
        await_bytes(amp_v.at[pl.ds(0, 16)], amp_sem.at[b])

        def quad(q, _):
            ij = b * 16 + q * 8
            x = amp_v[pl.ds(ij, 8)].reshape(512, 640)
            v = jnp.dot(x, w_b[...], preferred_element_type=F32) + x.astype(F32)
            for e in range(8):
                label = pirr[ij + e]
                at = pl.ds((q * 8 + e) * 65, 64)
                for k in range(5):
                    cols = slice(k * 128, (k + 1) * 128)
                    y_stage[k, at, :] = jnp.where(irr_x[:, cols] == label, v[e * 64 : (e + 1) * 64, cols], 0.0)
            return 0

        lax.fori_loop(0, 2, quad, 0)

        def turn(c, _):
            at = pl.ds(pl.multiple_of(b * 16, 16), 16)
            got = [y_stage[k, pl.ds(c * 8 + i, 16, stride=65), :].astype(BF16) for i in range(8) for k in range(5)]
            for i in range(40):
                dressed[c * 40 + i, at, :] = got[i]
            return 0

        lax.fori_loop(0, 8, turn, 0)
        return 0

    lax.fori_loop(0, 2, dress, 0)
    forward(0)
    lax.fori_loop(2, 4, dress, 0)

    def order(delta):
        def one(yy, _):
            first = (wrap(z + delta, NZ) * NY + yy) * 10
            for s in range(10):
                d_send[delta % 8, yy, :, s * 128 : (s + 1) * 128] = dressed[towners[r, first + s]]
            return 0

        lax.fori_loop(0, NY, one, 0)

    mine = pl.ds(pl.multiple_of(y * 64, 64), 64)

    def send(delta):
        order(delta)
        buf = d_send.at[delta % 8]
        if delta in FAR:
            to, sem = far.at[FAR[delta], mine], x_recv.at[FAR[delta]]
        else:
            to, sem = recv_f.at[NEAR[delta], mine], a_recv.at[NEAR[delta]]
        local(buf.at[y], to, sem)
        for k in (2, 1, 3):
            yy = wrap(y + k, NY)
            remote(buf.at[yy], to, a_send.at[delta % 8], sem, dev(z, yy, r))

    def sent(delta):
        await_bytes(d_send.at[0, pl.ds(0, NY - 1)], a_send.at[delta % 8])

    def go_on(delta):
        at = FAR[delta]
        await_bytes(far.at[at], x_recv.at[at])
        if delta == 4:
            for part in range(2):
                rows = pl.ds(part * 64, 64)
                remote(far.at[at, rows], recv_h.at[0, rows], x_send, a_recv.at[7 + part], dev(z + 2, y, r))
                low = pl.ds(128 + part * 64, 64)
                remote(far.at[at, low], recv_h.at[1, rows], x_send, a_recv.at[9 + part], dev(z - 2, y, r))
        else:
            remote(far.at[at], recv_f.at[3 + at], x_send, a_recv.at[3 + at], dev(z + 1 - 2 * at, y, r))

    for delta in WAY[:WINDOW]:
        send(delta)
    forward(1)

    diag64 = lax.broadcasted_iota(I32, (64, 128), 0) == lax.broadcasted_iota(I32, (64, 128), 1)
    for j in range(4):
        t = ltiles[j, pair]
        la, bb = oirr[lax.div(t, 5)], lax.rem(t, 5)
        lab = jnp.zeros((1, 128), I32)
        for k in range(5):
            lab = lab + jnp.where(bb == k, irow_ref[:, k * 128 : (k + 1) * 128], 0)
        lab = jnp.bitwise_xor(lab, la).astype(F32)
        for yy in range(NY):
            rowl = cyc_g[side, core, lax.div(r, 4), yy][20:21, 0:128].astype(F32)
            col = jnp.sum(jnp.where(diag64, jnp.broadcast_to(rowl, (64, 128)), 0.0), axis=1, keepdims=True)
            same = jnp.broadcast_to(col, (64, 128)) == lab
            keep[yy * 64 : (yy + 1) * 64, j * 128 : (j + 1) * 128] = jnp.where(same, 1.0, 0.0).astype(BF16)
    local(keep, keep_hbm, out_sem)

    def multiply(x, w, o):
        def cols(n, _):
            at = pl.ds(pl.multiple_of(n * 256, 256), 256)
            o[:, at] = jnp.dot(x[...], w[:, at], preferred_element_type=F32).astype(BF16)
            return 0

        lax.fori_loop(0, 2, cols, 0)

    def scatter(o, rr, n, sem):
        def piece(q):
            return o.at[pl.ds(pl.multiple_of(q * n, n), n)]

        for k in (4, 3, 5, 2, 6, 1, 7):
            q = wrap(r + k, NR)
            remote(piece(q), rr.at[r], r_send, sem, dev(z, y, q))
        local(piece(r), rr.at[r], sem)

    def reduce(item):
        if item < 7:
            (o, s), rr, fb, n = FULL[item], rr_f.at[item], fb_f.at[item], 32
            row = r * 32
        else:
            (o, s), rr, fb, n = HALF[item - 7], rr_h.at[item - 7], fb_h.at[item - 7], 16
            row = r * 16 + (item - 7) * 128
        await_bytes(rr, r_recv.at[item])
        total = rr[0].astype(F32)
        for q in range(1, NR):
            total = total + rr[q].astype(F32)
        fb[...] = total.astype(BF16)
        rows = out_hbm.at[pl.ds(pl.multiple_of(row, 16), n)]
        level = wrap(z + s, NZ)
        if item == 0:

            @pl.when(level == r)
            def _():
                local(fb, rows, f_recv)

            @pl.when(level != r)
            def _():
                remote(fb, rows, f_send.at[0], f_recv, dev(z + o, y, level))
        else:
            remote(fb, rows, f_send.at[1], f_recv, dev(z + o, y, level))

    ready = {2}

    def half_step(item, part):
        h, rows = item - 7, pl.ds(part * 64, 64)
        await_bytes(recv_h.at[h, rows], a_recv.at[7 + 2 * h + part])
        multiply(recv_h.at[h, rows], wbuf.at[HALF[h][0] + 2], ob_h.at[h, rows])

        def piece(q):
            return ob_h.at[h, pl.ds(pl.multiple_of(q * 16, 16), 16)]

        for k in (2, 1, 3):
            q = part * 4 + lax.rem(r + k, 4)
            remote(piece(q), rr_h.at[h, r], r_send, r_recv.at[item], dev(z, y, q))
        q = part * 4 + lax.rem(r, 4)

        @pl.when(q == r)
        def _():
            local(piece(r), rr_h.at[h, r], r_recv.at[item])

        @pl.when(q != r)
        def _():
            remote(piece(q), rr_h.at[h, r], r_send, r_recv.at[item], dev(z, y, q))

    def item_step(item):
        o, x, ob, rr, n = FULL[item][0], recv_f.at[item], ob_f.at[item], rr_f.at[item], 32
        if item == 0:
            await_bytes(wbuf.at[2], own_sem)
        if o in (2, -2) and o + 2 not in ready:
            ready.add(o + 2)
            for h in range(2):
                await_bytes(wbuf.at[o + 2, pl.ds(h * 640, 640)], w_recv.at[o + 2, h])
        await_bytes(x, a_recv.at[item])
        multiply(x, wbuf.at[o + 2], ob)
        scatter(ob, rr, n, r_recv.at[item])

    pending = []
    for i, delta in enumerate(WAY):
        if i + WINDOW < 8:
            sent(delta)
            send(WAY[i + WINDOW])
        if delta in FAR:
            go_on(delta)
            continue
        for item in TODO[delta]:
            item_step(item)
            if len(pending) > 1:
                reduce(pending.pop(0))
            pending.append(item)
    for part in range(2):
        for item in (7, 8):
            half_step(item, part)
    for item in (*pending, 7, 8):
        reduce(item)

    await_bytes(out_hbm, f_recv)

    @pl.when(sends)
    def _():
        await_bytes(cyc_g.at[0, 0, 0], c_send.at[0])
        await_bytes(cyc_g.at[0, 0, 0, pl.ds(0, 3)], c_send.at[0])

    await_bytes(cyc_g.at[0, 0, :, pl.ds(0, NY - 1)], c_send.at[1])
    await_bytes(cyc_g.at[0, 0], c_send.at[2])
    await_bytes(cyc_g.at[:, 0], c_send.at[3])
    await_bytes(wbuf.at[pl.ds(0, 4)], w_send)
    for delta in WAY[8 - WINDOW :]:
        sent(delta)
    await_bytes(far, x_send)
    await_bytes(rr_f.at[:, pl.ds(0, NR - 1)], r_send)
    await_bytes(rr_h.at[:, pl.ds(0, NR - 1)], r_send)

    @pl.when(z != r)
    def _():
        await_bytes(fb_f.at[0], f_send.at[0])

    await_bytes(fb_f.at[pl.ds(0, 6)], f_send.at[1])
    await_bytes(fb_h, f_send.at[1])
    pltpu.make_async_copy(keep, keep_hbm, out_sem).wait()


def shards(amplitudes, cycle_integrals, ladder_integrals, orbital_irrep, pair_irrep, tile_owners, ladder_tiles):
    hbm = pl.BlockSpec(memory_space=pltpu.MemorySpace.HBM)
    dma = pltpu.SemaphoreType.DMA
    out, keep = pl.pallas_call(
        kernel,
        out_shape=[pltpu.VMEM((256, 512), BF16)] * 2,
        in_specs=[hbm] * 7,
        out_specs=[pl.BlockSpec(memory_space=pltpu.MemorySpace.VMEM)] * 2,
        scratch_shapes=[
            pltpu.VMEM((20, 640), BF16),
            pltpu.VMEM((640,), I32),
            pltpu.VMEM((64,), I32),
            pltpu.SMEM((8, 320), I32),
            pltpu.SMEM((4, 32), I32),
            pltpu.SMEM((640,), I32),
            pltpu.SMEM((64,), I32),
            pltpu.VMEM((256, 512), BF16),
            pltpu.VMEM((64, 64, 640), BF16),
            pltpu.VMEM((24, 640), BF16),
            pltpu.VMEM((2, 2, 2, 4, 24, 640), BF16),
            pltpu.VMEM((640, 640), F32),
            pltpu.VMEM((640, 640), BF16),
            pltpu.VMEM((1, 640), I32),
            pltpu.VMEM((64, 640), I32),
            pltpu.VMEM((640, 128), I32),
            pltpu.VMEM((5, 1152, 128), F32),
            pltpu.VMEM((320, 64, 128), BF16),
            pltpu.VMEM((8, 4, 64, 1280), BF16),
            pltpu.VMEM((7, 256, 1280), BF16),
            pltpu.VMEM((2, 128, 1280), BF16),
            pltpu.VMEM((3, 256, 1280), BF16),
            pltpu.VMEM((5, 1280, 512), BF16),
            pltpu.VMEM((7, 256, 512), BF16),
            pltpu.VMEM((2, 128, 512), BF16),
            pltpu.VMEM((7, 8, 32, 512), BF16),
            pltpu.VMEM((2, 8, 16, 512), BF16),
            pltpu.VMEM((7, 32, 512), BF16),
            pltpu.VMEM((2, 16, 512), BF16),
            dma((7,)),
            dma,
            dma((4,)),
            dma,
            dma((4,)),
            dma((4,)),
            dma,
            dma((5, 2)),
            dma((8,)),
            dma((11,)),
            dma,
            dma((3,)),
            dma,
            dma((9,)),
            dma((2,)),
            dma,
        ],
        compiler_params=pltpu.CompilerParams(
            collective_id=0, has_side_effects=True, vmem_limit_bytes=56 << 20
        ),
        name="ladder",
    )(
        amplitudes,
        cycle_integrals,
        ladder_integrals.reshape(1280, 512),
        tile_owners,
        ladder_tiles.T,
        orbital_irrep,
        pair_irrep,
    )
    return jnp.where(keep != 0, out, jnp.zeros((), BF16))[None]


def solution(mesh):
    return jax.shard_map(
        shards,
        mesh=mesh,
        in_specs=(
            P("pair", "red", None),
            P("pair", None),
            P("pair", "red", None, None),
            P(),
            P("pair"),
            P(),
            P(),
        ),
        out_specs=P("pair", "red", None),
        check_vma=False,
    )
```

```python
import jax
import jax.numpy as jnp
from jax import lax
from jax.experimental import pallas as pl
from jax.experimental.pallas import tpu as pltpu
from jax.sharding import PartitionSpec as P

NZ, NY, NR = 8, 4, 8
F32, BF16, I32 = jnp.float32, jnp.bfloat16, jnp.int32
FULL = ((0, 0), (1, 0), (-1, 0), (2, -1), (-2, 1), (2, 0), (-2, 0))
HALF = ((2, -2), (-2, 2))
WAY = (0, 3, -3, 4, 1, -1, 2, -2)
NEAR = {0: 0, 1: 1, -1: 2, 2: 5, -2: 6}
FAR = {3: 0, -3: 1, 4: 2}
TODO = {0: (0,), 1: (1,), -1: (2,), 2: (3, 4, 5), -2: (6,)}
WINDOW = 3


def wrap(v, n):
    return lax.rem(v + n, n)


def kernel(
    amp_hbm, cyc_hbm, lad_hbm, to_hbm, lt_hbm, oi_hbm, pi_hbm,
    out_hbm, keep_hbm,
    cyc_in, orow, prow, towners, ltiles, oirr, pirr, keep,
    amp_v, cyc_ref, cyc_g, w_stage, w_b, irow_ref, irr_x, irr_c, y_stage, dressed, d_send,
    recv_f, recv_h, far, wbuf, ob_f, ob_h, rr_f, rr_h, fb_f, fb_h,
    in_sem, out_sem, amp_sem, own_sem, c_send, c_recv, w_send, w_recv, a_send, a_recv,
    x_send, x_recv, r_send, r_recv, f_send, f_recv,
):
    pair = lax.axis_index("pair")
    r = lax.axis_index("red")
    z, y = lax.div(pair, NY), lax.rem(pair, NY)

    def dev(zz, yy, rr):
        return (wrap(zz, NZ) * NY + wrap(yy, NY), wrap(rr, NR))

    def remote(src, dst, ssem, rsem, where):
        pltpu.make_async_remote_copy(
            src_ref=src, dst_ref=dst, send_sem=ssem, recv_sem=rsem,
            device_id=where, device_id_type=pl.DeviceIdType.MESH,
        ).start()

    def local(src, dst, sem):
        pltpu.make_async_copy(src, dst, sem).start()

    def await_bytes(ref, sem):
        pltpu.make_async_copy(ref, ref, sem).wait()

    bar = pltpu.get_barrier_semaphore()

    def greet(where):
        pl.semaphore_signal(bar, inc=1, device_id=where, device_id_type=pl.DeviceIdType.MESH)

    for k in (1, 7, 2, 6, 3, 5, 4):
        greet(dev(z + k, y, r))
    for k in range(1, NR):
        greet(dev(z, y, r + k))
    for k in range(1, NY):
        greet(dev(z, y + k, r))
    small = (
        (cyc_hbm, cyc_in), (oi_hbm, orow), (pi_hbm, prow), (to_hbm, towners),
        (lt_hbm, ltiles), (oi_hbm, oirr), (pi_hbm, pirr),
    )
    for i, (src, dst) in enumerate(small):
        local(src, dst, in_sem.at[i])
    for i, (src, dst) in enumerate(small):
        pltpu.make_async_copy(src, dst, in_sem.at[i]).wait()
    for k in range(5):
        irow_ref[:, k * 128 : (k + 1) * 128] = orow[pl.ds(k * 128, 128)].reshape(1, 128)
    cyc_ref[0:20, :] = cyc_in[...]
    cyc_ref[20:24, :] = jnp.zeros((4, 640), BF16)
    cyc_ref[20:24, 0:64] = jnp.broadcast_to(prow[...].reshape(1, 64), (4, 64)).astype(BF16)
    pl.semaphore_wait(bar, 2 * (NZ - 1) + NY - 1)

    side, core = lax.div(r, 2), lax.rem(r, 2)
    sends = z == r

    @pl.when(sends)
    def _():
        to = cyc_g.at[side, core, y]
        local(cyc_ref, to, c_recv.at[0])
        for k in (4, 3, 5, 2, 6, 1, 7):
            remote(cyc_ref, to, c_send.at[0], c_recv.at[0], dev(z + k, y, r))

    for h in range(2):
        rows = pl.ds(h * 640, 640)
        remote(lad_hbm.at[rows], wbuf.at[1, rows], w_send, w_recv.at[1, h], dev(z + 1, y, r))
        remote(lad_hbm.at[rows], wbuf.at[3, rows], w_send, w_recv.at[3, h], dev(z - 1, y, r))

    for b in range(4):
        rows = pl.ds(b * 16, 16)
        local(amp_hbm.at[rows], amp_v.at[rows], amp_sem.at[b])
    local(lad_hbm, wbuf.at[2], own_sem)

    diag = lax.broadcasted_iota(I32, (128, 128), 0) == lax.broadcasted_iota(I32, (128, 128), 1)
    for k in range(5):
        lab = jnp.broadcast_to(irow_ref[:, k * 128 : (k + 1) * 128], (128, 128))
        col = jnp.sum(jnp.where(diag, lab, 0), axis=1, keepdims=True)
        irr_c[k * 128 : (k + 1) * 128, :] = jnp.broadcast_to(col, (128, 128))
    slab = irr_c[pl.ds(pl.multiple_of(r * 64, 64), 64), :]
    for k in range(5):
        irr_x[:, k * 128 : (k + 1) * 128] = jnp.bitwise_xor(slab, irow_ref[:, k * 128 : (k + 1) * 128])

    part = cyc_g.at[side, core, y]
    await_bytes(part, c_recv.at[0])
    for k in (2, 1, 3):
        remote(part, part, c_send.at[1], c_recv.at[1], dev(z, y + k, r))
    await_bytes(cyc_g.at[0, 0, pl.ds(0, NY - 1)], c_recv.at[1])
    part = cyc_g.at[side, core]
    for k in (2, 1, 3):
        remote(part, part, c_send.at[2], c_recv.at[2], dev(z, y, r + 2 * k))
    partner = dev(z, y, r + 1 - 2 * core)
    remote(part, part, c_send.at[3], c_recv.at[3], partner)
    await_bytes(cyc_g.at[pl.ds(0, 3), 0], c_recv.at[2])
    for k in range(1, 4):
        part = cyc_g.at[lax.rem(side + k, 4), core]
        remote(part, part, c_send.at[3], c_recv.at[3], partner)
    await_bytes(cyc_g.at[:, 0], c_recv.at[3])

    def forward(h):
        rows = pl.ds(h * 640, 640)
        for a, b, dz in ((1, 0, 1), (3, 4, -1)):
            await_bytes(wbuf.at[a, rows], w_recv.at[a, h])
            remote(wbuf.at[a, rows], wbuf.at[b, rows], w_send, w_recv.at[b, h], dev(z + dz, y, r))

    for p in range(NZ * NY):
        w_stage[p * 20 : p * 20 + 20, :] = cyc_g[p // NY // 2, p // NY % 2, p % NY][:20, :].astype(F32)

    def mask_w(c, _):
        rows = pl.ds(pl.multiple_of(c * 128, 128), 128)
        for k in range(5):
            cols = slice(k * 128, (k + 1) * 128)
            keep = irr_c[rows, :] == irow_ref[:, cols]
            w_b[rows, cols] = jnp.where(keep, w_stage[rows, cols], 0.0).astype(BF16)
        return 0

    lax.fori_loop(0, 5, mask_w, 0)

    def dress(b, _):
        await_bytes(amp_v.at[pl.ds(0, 16)], amp_sem.at[b])

        def quad(q, _):
            ij = b * 16 + q * 8
            x = amp_v[pl.ds(ij, 8)].reshape(512, 640)
            v = jnp.dot(x, w_b[...], preferred_element_type=F32) + x.astype(F32)
            for e in range(8):
                label = pirr[ij + e]
                at = pl.ds((q * 8 + e) * 65, 64)
                for k in range(5):
                    cols = slice(k * 128, (k + 1) * 128)
                    y_stage[k, at, :] = jnp.where(irr_x[:, cols] == label, v[e * 64 : (e + 1) * 64, cols], 0.0)
            return 0

        lax.fori_loop(0, 2, quad, 0)

        def turn(c, _):
            at = pl.ds(pl.multiple_of(b * 16, 16), 16)
            got = [y_stage[k, pl.ds(c * 8 + i, 16, stride=65), :].astype(BF16) for i in range(8) for k in range(5)]
            for i in range(40):
                dressed[c * 40 + i, at, :] = got[i]
            return 0

        lax.fori_loop(0, 8, turn, 0)
        return 0

    lax.fori_loop(0, 2, dress, 0)
    forward(0)
    lax.fori_loop(2, 4, dress, 0)

    def order(delta):
        def one(yy, _):
            first = (wrap(z + delta, NZ) * NY + yy) * 10
            for s in range(10):
                d_send[delta % 8, yy, :, s * 128 : (s + 1) * 128] = dressed[towners[r, first + s]]
            return 0

        lax.fori_loop(0, NY, one, 0)

    mine = pl.ds(pl.multiple_of(y * 64, 64), 64)

    def send(delta):
        order(delta)
        buf = d_send.at[delta % 8]
        if delta in FAR:
            to, sem = far.at[FAR[delta], mine], x_recv.at[FAR[delta]]
        else:
            to, sem = recv_f.at[NEAR[delta], mine], a_recv.at[NEAR[delta]]
        local(buf.at[y], to, sem)
        for k in (2, 1, 3):
            yy = wrap(y + k, NY)
            remote(buf.at[yy], to, a_send.at[delta % 8], sem, dev(z, yy, r))

    def sent(delta):
        await_bytes(d_send.at[0, pl.ds(0, NY - 1)], a_send.at[delta % 8])

    def go_on(delta):
        at = FAR[delta]
        await_bytes(far.at[at], x_recv.at[at])
        if delta == 4:
            for part in range(2):
                rows = pl.ds(part * 64, 64)
                remote(far.at[at, rows], recv_h.at[0, rows], x_send, a_recv.at[7 + part], dev(z + 2, y, r))
                low = pl.ds(128 + part * 64, 64)
                remote(far.at[at, low], recv_h.at[1, rows], x_send, a_recv.at[9 + part], dev(z - 2, y, r))
        else:
            remote(far.at[at], recv_f.at[3 + at], x_send, a_recv.at[3 + at], dev(z + 1 - 2 * at, y, r))

    for delta in WAY[:WINDOW]:
        send(delta)
    forward(1)

    diag64 = lax.broadcasted_iota(I32, (64, 128), 0) == lax.broadcasted_iota(I32, (64, 128), 1)
    for j in range(4):
        t = ltiles[j, pair]
        la, bb = oirr[lax.div(t, 5)], lax.rem(t, 5)
        lab = jnp.zeros((1, 128), I32)
        for k in range(5):
            lab = lab + jnp.where(bb == k, irow_ref[:, k * 128 : (k + 1) * 128], 0)
        lab = jnp.bitwise_xor(lab, la).astype(F32)
        for yy in range(NY):
            rowl = cyc_g[side, core, yy][20:21, 0:128].astype(F32)
            col = jnp.sum(jnp.where(diag64, jnp.broadcast_to(rowl, (64, 128)), 0.0), axis=1, keepdims=True)
            same = jnp.broadcast_to(col, (64, 128)) == lab
            keep[yy * 64 : (yy + 1) * 64, j * 128 : (j + 1) * 128] = jnp.where(same, 1.0, 0.0).astype(BF16)
    local(keep, keep_hbm, out_sem)

    def multiply(x, w, o):
        def cols(n, _):
            at = pl.ds(pl.multiple_of(n * 256, 256), 256)
            o[:, at] = jnp.dot(x[...], w[:, at], preferred_element_type=F32).astype(BF16)
            return 0

        lax.fori_loop(0, 2, cols, 0)

    def scatter(o, rr, n, sem):
        def piece(q):
            return o.at[pl.ds(pl.multiple_of(q * n, n), n)]

        for k in (4, 3, 5, 2, 6, 1, 7):
            q = wrap(r + k, NR)
            remote(piece(q), rr.at[r], r_send, sem, dev(z, y, q))
        local(piece(r), rr.at[r], sem)

    def reduce(item):
        if item < 7:
            (o, s), rr, fb, n = FULL[item], rr_f.at[item], fb_f.at[item], 32
            row = r * 32
        else:
            (o, s), rr, fb, n = HALF[item - 7], rr_h.at[item - 7], fb_h.at[item - 7], 16
            row = r * 16 + (item - 7) * 128
        await_bytes(rr, r_recv.at[item])
        total = rr[0].astype(F32)
        for q in range(1, NR):
            total = total + rr[q].astype(F32)
        fb[...] = total.astype(BF16)
        rows = out_hbm.at[pl.ds(pl.multiple_of(row, 16), n)]
        level = wrap(z + s, NZ)
        if item == 0:

            @pl.when(level == r)
            def _():
                local(fb, rows, f_recv)

            @pl.when(level != r)
            def _():
                remote(fb, rows, f_send.at[0], f_recv, dev(z + o, y, level))
        else:
            remote(fb, rows, f_send.at[1], f_recv, dev(z + o, y, level))

    ready = {2}

    def half_step(item, part):
        h, rows = item - 7, pl.ds(part * 64, 64)
        await_bytes(recv_h.at[h, rows], a_recv.at[7 + 2 * h + part])
        multiply(recv_h.at[h, rows], wbuf.at[HALF[h][0] + 2], ob_h.at[h, rows])

        def piece(q):
            return ob_h.at[h, pl.ds(pl.multiple_of(q * 16, 16), 16)]

        for k in (2, 1, 3):
            q = part * 4 + lax.rem(r + k, 4)
            remote(piece(q), rr_h.at[h, r], r_send, r_recv.at[item], dev(z, y, q))
        q = part * 4 + lax.rem(r, 4)

        @pl.when(q == r)
        def _():
            local(piece(r), rr_h.at[h, r], r_recv.at[item])

        @pl.when(q != r)
        def _():
            remote(piece(q), rr_h.at[h, r], r_send, r_recv.at[item], dev(z, y, q))

    def item_step(item):
        o, x, ob, rr, n = FULL[item][0], recv_f.at[item], ob_f.at[item], rr_f.at[item], 32
        if item == 0:
            await_bytes(wbuf.at[2], own_sem)
        if o in (2, -2) and o + 2 not in ready:
            ready.add(o + 2)
            for h in range(2):
                await_bytes(wbuf.at[o + 2, pl.ds(h * 640, 640)], w_recv.at[o + 2, h])
        await_bytes(x, a_recv.at[item])
        multiply(x, wbuf.at[o + 2], ob)
        scatter(ob, rr, n, r_recv.at[item])

    pending = []
    for i, delta in enumerate(WAY):
        if i + WINDOW < 8:
            sent(delta)
            send(WAY[i + WINDOW])
        if delta in FAR:
            go_on(delta)
            continue
        for item in TODO[delta]:
            item_step(item)
            if len(pending) > 1:
                reduce(pending.pop(0))
            pending.append(item)
    for part in range(2):
        for item in (7, 8):
            half_step(item, part)
    for item in (*pending, 7, 8):
        reduce(item)

    await_bytes(out_hbm, f_recv)

    @pl.when(sends)
    def _():
        await_bytes(cyc_g.at[0, 0], c_send.at[0])
        await_bytes(cyc_g.at[0, 1, pl.ds(0, 3)], c_send.at[0])

    await_bytes(cyc_g.at[0, 0, pl.ds(0, NY - 1)], c_send.at[1])
    await_bytes(cyc_g.at[pl.ds(0, 3), 0], c_send.at[2])
    await_bytes(cyc_g.at[:, 0], c_send.at[3])
    await_bytes(wbuf.at[pl.ds(0, 4)], w_send)
    for delta in WAY[8 - WINDOW :]:
        sent(delta)
    await_bytes(far, x_send)
    await_bytes(rr_f.at[:, pl.ds(0, NR - 1)], r_send)
    await_bytes(rr_h.at[:, pl.ds(0, NR - 1)], r_send)

    @pl.when(z != r)
    def _():
        await_bytes(fb_f.at[0], f_send.at[0])

    await_bytes(fb_f.at[pl.ds(0, 6)], f_send.at[1])
    await_bytes(fb_h, f_send.at[1])
    pltpu.make_async_copy(keep, keep_hbm, out_sem).wait()


def shards(amplitudes, cycle_integrals, ladder_integrals, orbital_irrep, pair_irrep, tile_owners, ladder_tiles):
    hbm = pl.BlockSpec(memory_space=pltpu.MemorySpace.HBM)
    dma = pltpu.SemaphoreType.DMA
    out, keep = pl.pallas_call(
        kernel,
        out_shape=[pltpu.VMEM((256, 512), BF16)] * 2,
        in_specs=[hbm] * 7,
        out_specs=[pl.BlockSpec(memory_space=pltpu.MemorySpace.VMEM)] * 2,
        scratch_shapes=[
            pltpu.VMEM((20, 640), BF16),
            pltpu.VMEM((640,), I32),
            pltpu.VMEM((64,), I32),
            pltpu.SMEM((8, 320), I32),
            pltpu.SMEM((4, 32), I32),
            pltpu.SMEM((640,), I32),
            pltpu.SMEM((64,), I32),
            pltpu.VMEM((256, 512), BF16),
            pltpu.VMEM((64, 64, 640), BF16),
            pltpu.VMEM((24, 640), BF16),
            pltpu.VMEM((4, 2, 4, 24, 640), BF16),
            pltpu.VMEM((640, 640), F32),
            pltpu.VMEM((640, 640), BF16),
            pltpu.VMEM((1, 640), I32),
            pltpu.VMEM((64, 640), I32),
            pltpu.VMEM((640, 128), I32),
            pltpu.VMEM((5, 1152, 128), F32),
            pltpu.VMEM((320, 64, 128), BF16),
            pltpu.VMEM((8, 4, 64, 1280), BF16),
            pltpu.VMEM((7, 256, 1280), BF16),
            pltpu.VMEM((2, 128, 1280), BF16),
            pltpu.VMEM((3, 256, 1280), BF16),
            pltpu.VMEM((5, 1280, 512), BF16),
            pltpu.VMEM((7, 256, 512), BF16),
            pltpu.VMEM((2, 128, 512), BF16),
            pltpu.VMEM((7, 8, 32, 512), BF16),
            pltpu.VMEM((2, 8, 16, 512), BF16),
            pltpu.VMEM((7, 32, 512), BF16),
            pltpu.VMEM((2, 16, 512), BF16),
            dma((7,)),
            dma,
            dma((4,)),
            dma,
            dma((4,)),
            dma((4,)),
            dma,
            dma((5, 2)),
            dma((8,)),
            dma((11,)),
            dma,
            dma((3,)),
            dma,
            dma((9,)),
            dma((2,)),
            dma,
        ],
        compiler_params=pltpu.CompilerParams(
            collective_id=0, has_side_effects=True, vmem_limit_bytes=56 << 20
        ),
        name="ladder",
    )(
        amplitudes,
        cycle_integrals,
        ladder_integrals.reshape(1280, 512),
        tile_owners,
        ladder_tiles.T,
        orbital_irrep,
        pair_irrep,
    )
    return jnp.where(keep != 0, out, jnp.zeros((), BF16))[None]


def solution(mesh):
    return jax.shard_map(
        shards,
        mesh=mesh,
        in_specs=(
            P("pair", "red", None),
            P("pair", None),
            P("pair", "red", None, None),
            P(),
            P("pair"),
            P(),
            P(),
        ),
        out_specs=P("pair", "red", None),
        check_vma=False,
    )
```

```python
import jax
import jax.numpy as jnp
from jax import lax
from jax.experimental import pallas as pl
from jax.experimental.pallas import tpu as pltpu
from jax.sharding import PartitionSpec as P

NZ, NY, NR = 8, 4, 8
F32, BF16, I32 = jnp.float32, jnp.bfloat16, jnp.int32
FULL = ((0, 0), (1, 0), (-1, 0), (2, -1), (-2, 1), (2, 0), (-2, 0))
HALF = ((2, -2), (-2, 2))
WAY = (0, 3, -3, 4, 1, -1, 2, -2)
NEAR = {0: 0, 1: 1, -1: 2, 2: 5, -2: 6}
FAR = {3: 0, -3: 1, 4: 2}
TODO = {0: (0,), 1: (1,), -1: (2,), 2: (3, 4, 5), -2: (6,)}
WINDOW = 4


def wrap(v, n):
    return lax.rem(v + n, n)


def kernel(
    amp_hbm, cyc_hbm, lad_hbm, to_hbm, lt_hbm, oi_hbm, pi_hbm,
    out_hbm, keep_hbm,
    cyc_in, orow, prow, towners, ltiles, oirr, pirr, keep,
    amp_v, cyc_ref, cyc_g, w_stage, w_b, irow_ref, irr_x, irr_c, y_stage, dressed, d_send,
    recv_f, recv_h, far, wbuf, ob_f, ob_h, rr_f, rr_h, fb_f, fb_h,
    in_sem, out_sem, amp_sem, own_sem, c_send, c_recv, w_send, w_recv, a_send, a_recv,
    x_send, x_recv, r_send, r_recv, f_send, f_recv,
):
    pair = lax.axis_index("pair")
    r = lax.axis_index("red")
    z, y = lax.div(pair, NY), lax.rem(pair, NY)

    def dev(zz, yy, rr):
        return (wrap(zz, NZ) * NY + wrap(yy, NY), wrap(rr, NR))

    def remote(src, dst, ssem, rsem, where):
        pltpu.make_async_remote_copy(
            src_ref=src, dst_ref=dst, send_sem=ssem, recv_sem=rsem,
            device_id=where, device_id_type=pl.DeviceIdType.MESH,
        ).start()

    def local(src, dst, sem):
        pltpu.make_async_copy(src, dst, sem).start()

    def await_bytes(ref, sem):
        pltpu.make_async_copy(ref, ref, sem).wait()

    bar = pltpu.get_barrier_semaphore()

    def greet(where):
        pl.semaphore_signal(bar, inc=1, device_id=where, device_id_type=pl.DeviceIdType.MESH)

    for k in (1, 7, 2, 6, 3, 5, 4):
        greet(dev(z + k, y, r))
    for k in range(1, NR):
        greet(dev(z, y, r + k))
    for k in range(1, NY):
        greet(dev(z, y + k, r))
    small = (
        (cyc_hbm, cyc_in), (oi_hbm, orow), (pi_hbm, prow), (to_hbm, towners),
        (lt_hbm, ltiles), (oi_hbm, oirr), (pi_hbm, pirr),
    )
    for i, (src, dst) in enumerate(small):
        local(src, dst, in_sem.at[i])
    for i, (src, dst) in enumerate(small):
        pltpu.make_async_copy(src, dst, in_sem.at[i]).wait()
    for k in range(5):
        irow_ref[:, k * 128 : (k + 1) * 128] = orow[pl.ds(k * 128, 128)].reshape(1, 128)
    cyc_ref[0:20, :] = cyc_in[...]
    cyc_ref[20:24, :] = jnp.zeros((4, 640), BF16)
    cyc_ref[20:24, 0:64] = jnp.broadcast_to(prow[...].reshape(1, 64), (4, 64)).astype(BF16)
    pl.semaphore_wait(bar, 2 * (NZ - 1) + NY - 1)

    side, core = lax.div(r, 2), lax.rem(r, 2)
    sends = z == r

    @pl.when(sends)
    def _():
        to = cyc_g.at[side, core, y]
        local(cyc_ref, to, c_recv.at[0])
        for k in (4, 3, 5, 2, 6, 1, 7):
            remote(cyc_ref, to, c_send.at[0], c_recv.at[0], dev(z + k, y, r))

    for h in range(2):
        rows = pl.ds(h * 640, 640)
        remote(lad_hbm.at[rows], wbuf.at[1, rows], w_send, w_recv.at[1, h], dev(z + 1, y, r))
        remote(lad_hbm.at[rows], wbuf.at[3, rows], w_send, w_recv.at[3, h], dev(z - 1, y, r))

    for b in range(4):
        rows = pl.ds(b * 16, 16)
        local(amp_hbm.at[rows], amp_v.at[rows], amp_sem.at[b])
    local(lad_hbm, wbuf.at[2], own_sem)

    diag = lax.broadcasted_iota(I32, (128, 128), 0) == lax.broadcasted_iota(I32, (128, 128), 1)
    for k in range(5):
        lab = jnp.broadcast_to(irow_ref[:, k * 128 : (k + 1) * 128], (128, 128))
        col = jnp.sum(jnp.where(diag, lab, 0), axis=1, keepdims=True)
        irr_c[k * 128 : (k + 1) * 128, :] = jnp.broadcast_to(col, (128, 128))
    slab = irr_c[pl.ds(pl.multiple_of(r * 64, 64), 64), :]
    for k in range(5):
        irr_x[:, k * 128 : (k + 1) * 128] = jnp.bitwise_xor(slab, irow_ref[:, k * 128 : (k + 1) * 128])

    part = cyc_g.at[side, core, y]
    await_bytes(part, c_recv.at[0])
    for k in (2, 1, 3):
        remote(part, part, c_send.at[1], c_recv.at[1], dev(z, y + k, r))
    await_bytes(cyc_g.at[0, 0, pl.ds(0, NY - 1)], c_recv.at[1])
    part = cyc_g.at[side, core]
    for k in (2, 1, 3):
        remote(part, part, c_send.at[2], c_recv.at[2], dev(z, y, r + 2 * k))
    partner = dev(z, y, r + 1 - 2 * core)
    remote(part, part, c_send.at[3], c_recv.at[3], partner)
    await_bytes(cyc_g.at[pl.ds(0, 3), 0], c_recv.at[2])
    for k in range(1, 4):
        part = cyc_g.at[lax.rem(side + k, 4), core]
        remote(part, part, c_send.at[3], c_recv.at[3], partner)
    await_bytes(cyc_g.at[:, 0], c_recv.at[3])

    def forward(h):
        rows = pl.ds(h * 640, 640)
        for a, b, dz in ((1, 0, 1), (3, 4, -1)):
            await_bytes(wbuf.at[a, rows], w_recv.at[a, h])
            remote(wbuf.at[a, rows], wbuf.at[b, rows], w_send, w_recv.at[b, h], dev(z + dz, y, r))

    for p in range(NZ * NY):
        w_stage[p * 20 : p * 20 + 20, :] = cyc_g[p // NY // 2, p // NY % 2, p % NY][:20, :].astype(F32)

    def mask_w(c, _):
        rows = pl.ds(pl.multiple_of(c * 128, 128), 128)
        for k in range(5):
            cols = slice(k * 128, (k + 1) * 128)
            keep = irr_c[rows, :] == irow_ref[:, cols]
            w_b[rows, cols] = jnp.where(keep, w_stage[rows, cols], 0.0).astype(BF16)
        return 0

    lax.fori_loop(0, 5, mask_w, 0)

    def dress(b, _):
        await_bytes(amp_v.at[pl.ds(0, 16)], amp_sem.at[b])

        def quad(q, _):
            ij = b * 16 + q * 8
            x = amp_v[pl.ds(ij, 8)].reshape(512, 640)
            v = jnp.dot(x, w_b[...], preferred_element_type=F32) + x.astype(F32)
            for e in range(8):
                label = pirr[ij + e]
                at = pl.ds((q * 8 + e) * 65, 64)
                for k in range(5):
                    cols = slice(k * 128, (k + 1) * 128)
                    y_stage[k, at, :] = jnp.where(irr_x[:, cols] == label, v[e * 64 : (e + 1) * 64, cols], 0.0)
            return 0

        lax.fori_loop(0, 2, quad, 0)

        def turn(c, _):
            at = pl.ds(pl.multiple_of(b * 16, 16), 16)
            got = [y_stage[k, pl.ds(c * 8 + i, 16, stride=65), :].astype(BF16) for i in range(8) for k in range(5)]
            for i in range(40):
                dressed[c * 40 + i, at, :] = got[i]
            return 0

        lax.fori_loop(0, 8, turn, 0)
        return 0

    lax.fori_loop(0, 2, dress, 0)
    forward(0)
    lax.fori_loop(2, 4, dress, 0)

    def order(delta):
        def one(yy, _):
            first = (wrap(z + delta, NZ) * NY + yy) * 10
            for s in range(10):
                d_send[delta % 8, yy, :, s * 128 : (s + 1) * 128] = dressed[towners[r, first + s]]
            return 0

        lax.fori_loop(0, NY, one, 0)

    mine = pl.ds(pl.multiple_of(y * 64, 64), 64)

    def send(delta):
        order(delta)
        buf = d_send.at[delta % 8]
        if delta in FAR:
            to, sem = far.at[FAR[delta], mine], x_recv.at[FAR[delta]]
        else:
            to, sem = recv_f.at[NEAR[delta], mine], a_recv.at[NEAR[delta]]
        local(buf.at[y], to, sem)
        for k in (2, 1, 3):
            yy = wrap(y + k, NY)
            remote(buf.at[yy], to, a_send.at[delta % 8], sem, dev(z, yy, r))

    def sent(delta):
        await_bytes(d_send.at[0, pl.ds(0, NY - 1)], a_send.at[delta % 8])

    def go_on(delta):
        at = FAR[delta]
        await_bytes(far.at[at], x_recv.at[at])
        if delta == 4:
            for part in range(2):
                rows = pl.ds(part * 64, 64)
                remote(far.at[at, rows], recv_h.at[0, rows], x_send, a_recv.at[7 + part], dev(z + 2, y, r))
                low = pl.ds(128 + part * 64, 64)
                remote(far.at[at, low], recv_h.at[1, rows], x_send, a_recv.at[9 + part], dev(z - 2, y, r))
        else:
            remote(far.at[at], recv_f.at[3 + at], x_send, a_recv.at[3 + at], dev(z + 1 - 2 * at, y, r))

    for delta in WAY[:WINDOW]:
        send(delta)
    forward(1)

    diag64 = lax.broadcasted_iota(I32, (64, 128), 0) == lax.broadcasted_iota(I32, (64, 128), 1)
    for j in range(4):
        t = ltiles[j, pair]
        la, bb = oirr[lax.div(t, 5)], lax.rem(t, 5)
        lab = jnp.zeros((1, 128), I32)
        for k in range(5):
            lab = lab + jnp.where(bb == k, irow_ref[:, k * 128 : (k + 1) * 128], 0)
        lab = jnp.bitwise_xor(lab, la).astype(F32)
        for yy in range(NY):
            rowl = cyc_g[side, core, yy][20:21, 0:128].astype(F32)
            col = jnp.sum(jnp.where(diag64, jnp.broadcast_to(rowl, (64, 128)), 0.0), axis=1, keepdims=True)
            same = jnp.broadcast_to(col, (64, 128)) == lab
            keep[yy * 64 : (yy + 1) * 64, j * 128 : (j + 1) * 128] = jnp.where(same, 1.0, 0.0).astype(BF16)
    local(keep, keep_hbm, out_sem)

    def multiply(x, w, o):
        def cols(n, _):
            at = pl.ds(pl.multiple_of(n * 256, 256), 256)
            o[:, at] = jnp.dot(x[...], w[:, at], preferred_element_type=F32).astype(BF16)
            return 0

        lax.fori_loop(0, 2, cols, 0)

    def scatter(o, rr, n, sem):
        def piece(q):
            return o.at[pl.ds(pl.multiple_of(q * n, n), n)]

        for k in (4, 3, 5, 2, 6, 1, 7):
            q = wrap(r + k, NR)
            remote(piece(q), rr.at[r], r_send, sem, dev(z, y, q))
        local(piece(r), rr.at[r], sem)

    def reduce(item):
        if item < 7:
            (o, s), rr, fb, n = FULL[item], rr_f.at[item], fb_f.at[item], 32
            row = r * 32
        else:
            (o, s), rr, fb, n = HALF[item - 7], rr_h.at[item - 7], fb_h.at[item - 7], 16
            row = r * 16 + (item - 7) * 128
        await_bytes(rr, r_recv.at[item])
        total = rr[0].astype(F32)
        for q in range(1, NR):
            total = total + rr[q].astype(F32)
        fb[...] = total.astype(BF16)
        rows = out_hbm.at[pl.ds(pl.multiple_of(row, 16), n)]
        level = wrap(z + s, NZ)
        if item == 0:

            @pl.when(level == r)
            def _():
                local(fb, rows, f_recv)

            @pl.when(level != r)
            def _():
                remote(fb, rows, f_send.at[0], f_recv, dev(z + o, y, level))
        else:
            remote(fb, rows, f_send.at[1], f_recv, dev(z + o, y, level))

    ready = {2}

    def half_step(item, part):
        h, rows = item - 7, pl.ds(part * 64, 64)
        await_bytes(recv_h.at[h, rows], a_recv.at[7 + 2 * h + part])
        multiply(recv_h.at[h, rows], wbuf.at[HALF[h][0] + 2], ob_h.at[h, rows])

        def piece(q):
            return ob_h.at[h, pl.ds(pl.multiple_of(q * 16, 16), 16)]

        for k in (2, 1, 3):
            q = part * 4 + lax.rem(r + k, 4)
            remote(piece(q), rr_h.at[h, r], r_send, r_recv.at[item], dev(z, y, q))
        q = part * 4 + lax.rem(r, 4)

        @pl.when(q == r)
        def _():
            local(piece(r), rr_h.at[h, r], r_recv.at[item])

        @pl.when(q != r)
        def _():
            remote(piece(q), rr_h.at[h, r], r_send, r_recv.at[item], dev(z, y, q))

    def item_step(item):
        o, x, ob, rr, n = FULL[item][0], recv_f.at[item], ob_f.at[item], rr_f.at[item], 32
        if item == 0:
            await_bytes(wbuf.at[2], own_sem)
        if o in (2, -2) and o + 2 not in ready:
            ready.add(o + 2)
            for h in range(2):
                await_bytes(wbuf.at[o + 2, pl.ds(h * 640, 640)], w_recv.at[o + 2, h])
        await_bytes(x, a_recv.at[item])
        multiply(x, wbuf.at[o + 2], ob)
        scatter(ob, rr, n, r_recv.at[item])

    pending = []
    for i, delta in enumerate(WAY):
        if i + WINDOW < 8:
            sent(delta)
            send(WAY[i + WINDOW])
        if delta in FAR:
            go_on(delta)
            continue
        for item in TODO[delta]:
            item_step(item)
            if len(pending) > 1:
                reduce(pending.pop(0))
            pending.append(item)
    for part in range(2):
        for item in (7, 8):
            half_step(item, part)
    for item in (*pending, 7, 8):
        reduce(item)

    await_bytes(out_hbm, f_recv)

    @pl.when(sends)
    def _():
        await_bytes(cyc_g.at[0, 0], c_send.at[0])
        await_bytes(cyc_g.at[0, 1, pl.ds(0, 3)], c_send.at[0])

    await_bytes(cyc_g.at[0, 0, pl.ds(0, NY - 1)], c_send.at[1])
    await_bytes(cyc_g.at[pl.ds(0, 3), 0], c_send.at[2])
    await_bytes(cyc_g.at[:, 0], c_send.at[3])
    await_bytes(wbuf.at[pl.ds(0, 4)], w_send)
    for delta in WAY[8 - WINDOW :]:
        sent(delta)
    await_bytes(far, x_send)
    await_bytes(rr_f.at[:, pl.ds(0, NR - 1)], r_send)
    await_bytes(rr_h.at[:, pl.ds(0, NR - 1)], r_send)

    @pl.when(z != r)
    def _():
        await_bytes(fb_f.at[0], f_send.at[0])

    await_bytes(fb_f.at[pl.ds(0, 6)], f_send.at[1])
    await_bytes(fb_h, f_send.at[1])
    pltpu.make_async_copy(keep, keep_hbm, out_sem).wait()


def shards(amplitudes, cycle_integrals, ladder_integrals, orbital_irrep, pair_irrep, tile_owners, ladder_tiles):
    hbm = pl.BlockSpec(memory_space=pltpu.MemorySpace.HBM)
    dma = pltpu.SemaphoreType.DMA
    out, keep = pl.pallas_call(
        kernel,
        out_shape=[pltpu.VMEM((256, 512), BF16)] * 2,
        in_specs=[hbm] * 7,
        out_specs=[pl.BlockSpec(memory_space=pltpu.MemorySpace.VMEM)] * 2,
        scratch_shapes=[
            pltpu.VMEM((20, 640), BF16),
            pltpu.VMEM((640,), I32),
            pltpu.VMEM((64,), I32),
            pltpu.SMEM((8, 320), I32),
            pltpu.SMEM((4, 32), I32),
            pltpu.SMEM((640,), I32),
            pltpu.SMEM((64,), I32),
            pltpu.VMEM((256, 512), BF16),
            pltpu.VMEM((64, 64, 640), BF16),
            pltpu.VMEM((24, 640), BF16),
            pltpu.VMEM((4, 2, 4, 24, 640), BF16),
            pltpu.VMEM((640, 640), F32),
            pltpu.VMEM((640, 640), BF16),
            pltpu.VMEM((1, 640), I32),
            pltpu.VMEM((64, 640), I32),
            pltpu.VMEM((640, 128), I32),
            pltpu.VMEM((5, 1152, 128), F32),
            pltpu.VMEM((320, 64, 128), BF16),
            pltpu.VMEM((8, 4, 64, 1280), BF16),
            pltpu.VMEM((7, 256, 1280), BF16),
            pltpu.VMEM((2, 128, 1280), BF16),
            pltpu.VMEM((3, 256, 1280), BF16),
            pltpu.VMEM((5, 1280, 512), BF16),
            pltpu.VMEM((7, 256, 512), BF16),
            pltpu.VMEM((2, 128, 512), BF16),
            pltpu.VMEM((7, 8, 32, 512), BF16),
            pltpu.VMEM((2, 8, 16, 512), BF16),
            pltpu.VMEM((7, 32, 512), BF16),
            pltpu.VMEM((2, 16, 512), BF16),
            dma((7,)),
            dma,
            dma((4,)),
            dma,
            dma((4,)),
            dma((4,)),
            dma,
            dma((5, 2)),
            dma((8,)),
            dma((11,)),
            dma,
            dma((3,)),
            dma,
            dma((9,)),
            dma((2,)),
            dma,
        ],
        compiler_params=pltpu.CompilerParams(
            collective_id=0, has_side_effects=True, vmem_limit_bytes=56 << 20
        ),
        name="ladder",
    )(
        amplitudes,
        cycle_integrals,
        ladder_integrals.reshape(1280, 512),
        tile_owners,
        ladder_tiles.T,
        orbital_irrep,
        pair_irrep,
    )
    return jnp.where(keep != 0, out, jnp.zeros((), BF16))[None]


def solution(mesh):
    return jax.shard_map(
        shards,
        mesh=mesh,
        in_specs=(
            P("pair", "red", None),
            P("pair", None),
            P("pair", "red", None, None),
            P(),
            P("pair"),
            P(),
            P(),
        ),
        out_specs=P("pair", "red", None),
        check_vma=False,
    )
```
